512 devices in a mesh: wide: 64 (over z_lo, x, core), narrow: 8 (over y, z_hi).
Axes of the slice: x: 4, y: 4, z: 16 (z_hi: 2, z_lo: 8; z = z_hi * 8 + z_lo), core: 2. Of those that a mesh axis runs over, the one named last changes fastest.
Arguments:
- ice_x: float32 [1024, 10, 1024], P('wide', None, 'narrow'), may hold values from -6 to 6
- ice_y: float32 [1024, 10, 1024], P('wide', None, 'narrow'), may hold values from -6 to 6
- ice_temp: float32 [1024, 10, 1024], P('wide', None, 'narrow'), may hold values from -2 to 2
- ocean_x: float32 [1024, 80, 1024], P('wide', None, 'narrow'), may hold values from -6 to 6
- ocean_y: float32 [1024, 80, 1024], P('wide', None, 'narrow'), may hold values from -6 to 6
- ocean_temp: float32 [1024, 80, 1024], P('wide', None, 'narrow'), may hold values from -2 to 2
- thick: float32 [1024, 1024], P('wide', 'narrow'), may hold values from 1 to 10
- grounded_mask: int32 [1024, 1024], P('wide', 'narrow'), may hold values 0 or 1
- wet_mask: int32 [1024, 1024], P('wide', 'narrow'), may hold values 0 or 1
- ice_links: int32 [1024, 8], P('wide', 'narrow'), may hold values from -1 to 1023, as said below
- ocean_links: int32 [1024, 8], P('wide', 'narrow'), may hold values from -1 to 1023, as said below
Outputs:
- ice_state: float32 [3, 1024, 10, 1024], P(None, 'wide', None, 'narrow')
- ocean_state: float32 [3, 1024, 80, 1024], P(None, 'wide', None, 'narrow')
- thick_out: float32 [1024, 1024], P('wide', 'narrow')
- melt_out: float32 [1024, 1024], P('wide', 'narrow')
The draws below stay inside these ranges and needn't reach their ends.
Inputs may be any that keep to these rules, and one draw needn't show every extreme that they name: `ice_links`: within one column group an ice block names an ocean block exactly when that ocean block names it back. Per column group, for any ocean tile and ice tile, at most 1 block of the ocean tile names a block of the ice tile, and that bound is reached in every draw, as is an ocean tile with all 16 blocks linked. `ocean_links`: the mirror of ice_links, as described there.
All inputs are finite; a program needn't handle non-finite values. No bound on the sum of `grounded_mask` or of `wet_mask` on one device may be relied on, other than what follows from the above.
Results may differ from the reference program's by a relative error of at most 0.000071.
Values sent between devices are 32-bit elements; how exact they have to be, the bound alone decides.
A program may use at most 64 MiB of HBM per device.

```python
import math
import jax
import jax.numpy as jnp

TC = 128
LAYERS = 10
LEVELS = 80
PICARD = 2
NB = 16
CAP = 1
BR = 1
ROWS = 1024
COLS = 1024
N_WIDE = 64
N_NARROW = 8


def link_column(key):
    count = N_WIDE
    key_order, key_share, key_roll, key_anchor, key_slots = jax.random.split(key, 5)
    sigma = jax.random.permutation(key_order, count).astype(jnp.int32)
    share = 75 + jax.random.randint(key_share, (count,), 0, 26)
    rolled = jax.random.randint(key_roll, (count, NB), 0, 100)
    anchor = jax.random.randint(key_anchor, (), 0, count)
    forced = (anchor - sigma) % count < NB // CAP
    coupled = (rolled < share[:, None]) | forced[:, None]
    block_index = jnp.arange(NB, dtype=jnp.int32)
    offset = block_index // CAP
    target = (sigma[:, None] + offset[None, :]) % count
    perms = jax.vmap(lambda inner: jax.random.permutation(inner, NB))(jax.random.split(key_slots, count)).astype(jnp.int32)
    destination = target * NB + perms[target, jnp.broadcast_to(block_index[None, :], target.shape)]
    ice_side = jnp.where(coupled, destination, -1).astype(jnp.int32).reshape(-1)
    source = (jnp.arange(count, dtype=jnp.int32)[:, None] * NB + block_index[None, :]).astype(jnp.int32)
    ocean_side = jnp.full((count * NB,), -1, jnp.int32).at[destination.reshape(-1)].set(jnp.where(coupled, source, -1).reshape(-1).astype(jnp.int32))
    return jnp.stack([ice_side, ocean_side])


def link_tables(key):
    base = jax.random.fold_in(key, 7)
    return jax.vmap(link_column)(jax.random.split(base, N_NARROW))


def draw_ice_links(key, part):
    return link_tables(key)[:, 0, :].T.astype(jnp.int32)


def draw_ocean_links(key, part):
    return link_tables(key)[:, 1, :].T.astype(jnp.int32)


def plant(values, stream_key, low, high):
    longest = values.shape.index(max(values.shape))
    spots = []
    for shift in (0, 1):
        where = [jax.random.randint(jax.random.fold_in(stream_key, axis), (), 0, length) for axis, length in enumerate(values.shape)]
        where[longest] = (where[longest] + shift) % values.shape[longest]
        spots.append(tuple(where))
    return values.at[spots[0]].set(low).at[spots[1]].set(high)


def block_scale(key, shape, cuts, smallest, largest):
    def one(axis_at, blocks):
        steps = jax.random.uniform(jax.random.fold_in(jax.random.fold_in(key, 6), axis_at), (blocks,), jnp.float32, smallest / len(cuts), largest / len(cuts))
        return jnp.repeat(jnp.exp(steps), shape[axis_at] // blocks).reshape((-1,) + (1,) * (len(shape) - axis_at - 1))

    gain = one(*cuts[0])
    for cut in cuts[1:]:
        gain = gain * one(*cut)
    return gain


def centred(own_key, shape, width, most, cuts=(), kind=jnp.bfloat16):
    result = width * jax.random.normal(own_key, shape, jnp.float32)
    if cuts:
        result = result * block_scale(own_key, shape, cuts, -0.22, 0.18)
    return jnp.clip(result, -most, most).astype(kind)


def setup_inputs(seed: int = 0) -> dict:
    streams_of = jax.random.split(jax.random.key(seed), 12)
    return {
        "ice_x": centred(streams_of[0], (ROWS, LAYERS, COLS), 1.0, 6.0, ((0, 64), (2, 8)), jnp.float32),
        "ice_y": centred(streams_of[1], (ROWS, LAYERS, COLS), 1.0, 6.0, ((0, 64), (2, 8)), jnp.float32),
        "ice_temp": jnp.clip(jax.random.uniform(streams_of[2], (ROWS, LAYERS, COLS), jnp.float32, -2.0, 2.0) * block_scale(streams_of[2], (ROWS, LAYERS, COLS), ((0, 64), (2, 8)), -0.4, 0.0), -2.0, 2.0),
        "ocean_x": centred(streams_of[3], (ROWS, LEVELS, COLS), 1.0, 6.0, ((0, 64), (2, 8)), jnp.float32),
        "ocean_y": centred(streams_of[4], (ROWS, LEVELS, COLS), 1.0, 6.0, ((0, 64), (2, 8)), jnp.float32),
        "ocean_temp": jnp.clip(jax.random.uniform(streams_of[5], (ROWS, LEVELS, COLS), jnp.float32, -2.0, 2.0) * block_scale(streams_of[5], (ROWS, LEVELS, COLS), ((0, 64), (2, 8)), -0.4, 0.0), -2.0, 2.0),
        "thick": jnp.clip(jnp.exp(math.log(10.0) - 2.3025851 * jax.random.uniform(streams_of[6], (ROWS, COLS), jnp.float32) ** block_scale(streams_of[6], (ROWS, COLS), ((0, 64), (1, 8)), -0.2, 0.2)), 1.0, 10.0),
        "grounded_mask": plant((jax.random.randint(streams_of[7], (ROWS, COLS), 0, 2) < 1).astype(jnp.int32), jax.random.fold_in(streams_of[7], 1), 0, 1),
        "wet_mask": plant((jax.random.randint(streams_of[8], (ROWS, COLS), 0, 2) < 1).astype(jnp.int32), jax.random.fold_in(streams_of[8], 1), 0, 1),
        "ice_links": draw_ice_links(jax.random.fold_in(streams_of[11], 71), 0),
        "ocean_links": draw_ocean_links(jax.random.fold_in(streams_of[11], 71), 0),
    }


DIFFUSE = 0.2
GAMMA_MELT = 0.5
TIME_STEP = 0.05
SLOPE_SCALE = 0.1
STRAIN_FLOOR = 0.01
HEATING_RATE = 0.01


def to_blocks(field):
    count_rows = field.shape[0]
    return field.reshape(count_rows // BR, BR, N_NARROW, TC).transpose(0, 2, 1, 3)


def from_blocks(pieces):
    count = pieces.shape[0]
    return pieces.transpose(0, 2, 1, 3).reshape(count * BR, N_NARROW * TC)


def fetch(pieces, link_list):
    linked = (link_list >= 0).astype(jnp.float32)
    link_safe = jnp.maximum(link_list, 0).astype(jnp.int32)
    arrived = pieces[link_safe, jnp.arange(N_NARROW, dtype=jnp.int32)[None, :]]
    weight = jnp.broadcast_to(linked[:, :, None, None], arrived.shape)
    return from_blocks(arrived * weight), from_blocks(weight)


def apply_diffuse(field_pad, wet_pad):
    count_rows = field_pad.shape[0] - 2
    count_cols = field_pad.shape[2] - 2
    centre = field_pad[1:-1, :, 1:-1]
    wet_centre = wet_pad[1:-1, 1:-1]
    total = jnp.zeros_like(centre)
    for row_off, col_off in ((0, 1), (2, 1), (1, 0), (1, 2)):
        weight = wet_centre * wet_pad[row_off:row_off + count_rows, col_off:col_off + count_cols]
        total = total + weight[:, None, :] * (field_pad[row_off:row_off + count_rows, :, col_off:col_off + count_cols] - centre)
    return centre + DIFFUSE * total


def strains(padded):
    along_rows = 0.5 * (padded[2:, :, 1:-1] - padded[:-2, :, 1:-1])
    along_cols = 0.5 * (padded[1:-1, :, 2:] - padded[1:-1, :, :-2])
    middle = padded[1:-1, :, 1:-1]
    vertical = jnp.concatenate([middle[:, 1:, :] - middle[:, :-1, :], jnp.zeros_like(middle[:, :1, :])], axis=1)
    return along_rows, along_cols, vertical, middle


def layer_shift(field):
    zeros = jnp.zeros_like(field[:, :1, :])
    above = jnp.concatenate([field[:, 1:, :], zeros], axis=1)
    below = jnp.concatenate([zeros, field[:, :-1, :]], axis=1)
    return above + below


def picard(pad_x, pad_y, rate_factor, inside, stress_x, stress_y, friction):
    count_rows = pad_x.shape[0] - 4
    count_cols = pad_x.shape[2] - 4
    layers = pad_x.shape[1]
    ux, uy, uz, mid_x = strains(pad_x)
    vx, vy, vz, mid_y = strains(pad_y)
    eps2 = ux * ux + vy * vy + ux * vy + 0.25 * (uy + vx) ** 2 + 0.25 * (uz * uz + vz * vz)
    eta = rate_factor * (eps2 + STRAIN_FLOOR) ** (-1.0 / 3.0) * inside[:, None, :]
    centre = eta[1:-1, :, 1:-1]
    level = jnp.arange(layers)
    vertical_count = ((level > 0).astype(jnp.float32) + (level < layers - 1).astype(jnp.float32))[None, :, None]
    diagonal = centre * vertical_count + friction[:, None, :]
    sum_x = stress_x[:, None, :] + centre * layer_shift(mid_x[1:-1, :, 1:-1])
    sum_y = stress_y[:, None, :] + centre * layer_shift(mid_y[1:-1, :, 1:-1])
    for row_off, col_off in ((0, 1), (2, 1), (1, 0), (1, 2)):
        face = 0.5 * (centre + eta[row_off:row_off + count_rows, :, col_off:col_off + count_cols])
        diagonal = diagonal + face
        sum_x = sum_x + face * mid_x[row_off:row_off + count_rows, :, col_off:col_off + count_cols]
        sum_y = sum_y + face * mid_y[row_off:row_off + count_rows, :, col_off:col_off + count_cols]
    return sum_x / diagonal, sum_y / diagonal, centre * eps2[1:-1, :, 1:-1]


def reference(ice_x, ice_y, ice_temp, ocean_x, ocean_y, ocean_temp, thick, grounded_mask, wet_mask, ice_links, ocean_links):
    grounded = grounded_mask.astype(jnp.float32)
    wet = wet_mask.astype(jnp.float32)
    draft_field = 0.9 * thick * (1.0 - grounded)
    ocean_draft, coupled = fetch(to_blocks(draft_field), ocean_links)
    wet_pad = jnp.pad(wet, 1)
    pad_three = ((1, 1), (0, 0), (1, 1))
    ocean_heat = apply_diffuse(jnp.pad(ocean_temp, pad_three), wet_pad)
    current_x = apply_diffuse(jnp.pad(ocean_x, pad_three), wet_pad)
    current_y = apply_diffuse(jnp.pad(ocean_y, pad_three), wet_pad)
    freezing = 0.0832 - 0.761 * ocean_draft
    melt_rate = GAMMA_MELT * (ocean_heat[:, 0, :] - freezing) * wet * coupled
    ocean_heat = ocean_heat.at[:, 0, :].add(-0.2 * melt_rate)
    ice_melt, unused = fetch(to_blocks(melt_rate), ice_links)
    new_thick = thick - TIME_STEP * ice_melt * (1.0 - grounded)
    surface = new_thick * (0.1 + 0.9 * grounded)
    surface_pad = jnp.pad(surface, 1)
    stress_x = -SLOPE_SCALE * new_thick * 0.5 * (surface_pad[2:, 1:-1] - surface_pad[:-2, 1:-1])
    stress_y = -SLOPE_SCALE * new_thick * 0.5 * (surface_pad[1:-1, 2:] - surface_pad[1:-1, :-2])
    friction = 0.1 + 9.9 * grounded
    inside = jnp.pad(jnp.ones((ROWS, COLS), jnp.float32), 1)
    rate_factor = jnp.exp(0.25 * jnp.pad(ice_temp, pad_three))
    velocity_x = ice_x
    velocity_y = ice_y
    pad_two = ((2, 2), (0, 0), (2, 2))
    heating = jnp.zeros_like(velocity_x)
    for sweep_index in range(PICARD):
        velocity_x, velocity_y, heating = picard(jnp.pad(velocity_x, pad_two), jnp.pad(velocity_y, pad_two), rate_factor, inside, stress_x, stress_y, friction)
    ice_heat = ice_temp + HEATING_RATE * heating
    ice_state = jnp.stack([velocity_x, velocity_y, ice_heat])
    ocean_state = jnp.stack([current_x, current_y, ocean_heat])
    return ice_state, ocean_state, new_thick, melt_rate
```

```python
import functools

import jax
import jax.numpy as jnp
from jax import lax
from jax.experimental import pallas as pl
from jax.experimental.pallas import tpu as pltpu
from jax.sharding import PartitionSpec as P

MESH = pl.DeviceIdType.MESH
F32 = jnp.float32

ROWS = 16
LANES = 128
LAYERS = 10
GROUPS = 10
RING = 24
WIDTH = 256


def iota(shape, dim):
    return lax.broadcasted_iota(jnp.int32, shape, dim)


def pack_cols(pieces):
    lane = iota((ROWS, LANES), 1)
    row = iota((ROWS, LANES), 0)
    acc = jnp.zeros((ROWS, LANES), F32)
    for j, (value, col) in enumerate(pieces):
        wide = jnp.broadcast_to(value[:, col : col + 1], (ROWS, LANES))
        acc = jnp.where(lane == row + 16 * j, wide, acc)
    return jnp.sum(acc, axis=0, keepdims=True)


def unpack_col(mid, j):
    lane = iota((ROWS, LANES), 1)
    row = iota((ROWS, LANES), 0)
    wide = jnp.broadcast_to(mid, (ROWS, LANES))
    return jnp.sum(jnp.where(lane == row + 16 * j, wide, 0.0), axis=1, keepdims=True)


def unpack_rim(mid, below, above, j):
    lane = iota((8, LANES), 1)
    sub = iota((8, LANES), 0)
    edge = jnp.where(sub < 4, jnp.broadcast_to(below, (8, LANES)), jnp.broadcast_to(above, (8, LANES)))
    place = jnp.where(sub < 4, sub, sub + 8)
    outer = jnp.sum(jnp.where(lane == place + 16 * j, edge, 0.0), axis=1, keepdims=True)
    return jnp.concatenate([unpack_col(mid, j), outer], axis=0)


def ring_field(own, below, above, left, right):
    sub = iota((8, LANES), 0)
    main = jnp.concatenate([own, jnp.where(sub < 4, below, above)], axis=0)
    lane = iota((RING, LANES), 1)
    rim = jnp.zeros((RING, LANES), F32)
    for j in range(3):
        rim = jnp.where(lane == 125 + j, unpack_rim(*left, j), rim)
        rim = jnp.where(lane == j, unpack_rim(*right, j), rim)
    return jnp.concatenate([main, rim], axis=1)


def up(x):
    return pltpu.roll(x, 1, axis=0)


def down(x):
    return pltpu.roll(x, x.shape[0] - 1, axis=0)


def left_of(x):
    return pltpu.roll(x, 1, axis=1)


def right_of(x):
    return pltpu.roll(x, x.shape[1] - 1, axis=1)


def sweep(here, above, heat, is_last, is_first, inside, friction, rows, width):
    a, b = here
    has_above = 1.0 - is_last
    has_below = 1.0 - is_first
    (au, bu), (ad, bd) = above
    aN, aS, aW, aE = up(a), down(a), left_of(a), right_of(a)
    bN, bS, bW, bE = up(b), down(b), left_of(b), right_of(b)
    ux, uy = 0.5 * (aS - aN), 0.5 * (aE - aW)
    vx, vy = 0.5 * (bS - bN), 0.5 * (bE - bW)
    uz, vz = au - a, bu - b
    shear = uy + vx
    eps2 = ux * ux + vy * vy + ux * vy + 0.25 * (shear * shear) + 0.25 * (uz * uz + vz * vz)
    eta = jnp.exp(0.25 * heat - jnp.log(eps2 + 0.01) * (1.0 / 3.0)) * inside
    cut = lambda x: x[:rows, :width]
    c = cut(eta)
    diag = c * (has_above + has_below) + friction
    up_c, down_c = c * has_above, c * has_below
    sx = up_c * cut(au) + down_c * cut(ad)
    sy = up_c * cut(bu) + down_c * cut(bd)
    for e, x, y in (
        (up(eta), aN, bN),
        (down(eta), aS, bS),
        (left_of(eta), aW, bW),
        (right_of(eta), aE, bE),
    ):
        face = 0.5 * (c + cut(e))
        diag = diag + face
        sx = sx + face * cut(x)
        sy = sy + face * cut(y)
    return sx, sy, diag, c * cut(eps2)


def kernel(
    NW,
    NN,
    ice_x,
    ice_y,
    ice_t,
    oce_x,
    oce_y,
    oce_t,
    thick_ref,
    ground_ref,
    wet_ref,
    ice_links,
    ocean_links,
    ice_out,
    ocean_out,
    thick_out,
    melt_out,
    E,
    rowbuf,
    oc,
    ipack,
    irecv,
    opack,
    orecv,
    quilt,
    iquilt,
    msg,
    msg_recv,
    msg3,
    msg3_recv,
    gw_recv,
    t_recv,
    table,
    arrived,
    table2,
    arrived2,
    weights,
    SX,
    SY,
    RD,
    local_sem,
    near_send,
    near_recv,
    a2a_send,
    a2a_recv,
    a2a_send2,
    a2a_recv2,
):
    w = lax.axis_index("wide")
    n = lax.axis_index("narrow")
    wp, wm = lax.rem(w + 1, NW), lax.rem(w + NW - 1, NW)
    np_, nm = lax.rem(n + 1, NN), lax.rem(n + NN - 1, NN)
    wide_of = {-1: wm, 0: w, 1: wp}
    ices = (ice_x, ice_y, ice_t)
    oces = (oce_x, oce_y, oce_t)

    barrier = pltpu.get_barrier_semaphore()

    def greet(i, carry):
        pl.semaphore_signal(
            barrier, 1, device_id={"wide": lax.rem(w + i, NW), "narrow": n}, device_id_type=MESH
        )
        return carry

    lax.fori_loop(1, NW, greet, 0)
    for nb in (nm, np_):
        for dw in (-1, 0, 1):
            pl.semaphore_signal(
                barrier, 1, device_id={"wide": wide_of[dw], "narrow": nb}, device_id_type=MESH
            )

    loads = []
    for f in range(3):
        loads.append(pltpu.make_async_copy(oces[f], oc.at[pl.ds(f * 180 + 10, 160)], local_sem.at[f]))
    for f in range(3):
        loads.append(
            pltpu.make_async_copy(
                ices[f],
                E.at[pl.ds(f * LAYERS, LAYERS), pl.ds(0, ROWS), pl.ds(0, LANES)],
                local_sem.at[3 + f],
            )
        )
    for load in loads:
        load.start()

    grounded = ground_ref[...].astype(F32)
    wet = wet_ref[...].astype(F32)
    thick = thick_ref[...]
    draft = 0.9 * thick * (1.0 - grounded)

    def build_table(dst, values, links):
        dest = iota((NW, LANES), 0)
        acc = jnp.zeros((NW, LANES), F32)
        for q in range(ROWS):
            hit = dest == (links[q] >> 4)
            acc = jnp.where(hit, jnp.broadcast_to(values[q : q + 1, :], (NW, LANES)), acc)
        dst[...] = acc.reshape(NW, 1, LANES)

    def gather(src, links):
        rows = []
        for q in range(ROWS):
            link = links[q]
            row = src[jnp.maximum(link, 0) >> 4]
            rows.append(jnp.where(jnp.full((1, LANES), link, jnp.int32) >= 0, row, 0.0))
        return jnp.concatenate(rows, axis=0)

    build_table(table, draft, ice_links)
    arrived[w] = table[w]

    for load in loads[:3]:
        load.wait()
    t0 = jnp.concatenate([oc[360 + 10 + 10 * r, 0:1, :] for r in range(ROWS)], axis=0)
    msg[0] = pack_cols([(t0, 127), (wet, 127), (grounded, 125), (grounded, 126), (grounded, 127)])
    msg[1] = pack_cols([(t0, 0), (wet, 0), (grounded, 0), (grounded, 1), (grounded, 2)])

    lane8 = iota((8, LANES), 1)

    def pack_ocean(j, accs):
        out = []
        for v in range(8):
            k = v * 64 + j
            if v == 7:
                k = jnp.minimum(k, 479)
            x = oc[k + 20 * (k // 160) + 10]
            out.append(jnp.where((lane8 >> 1) == j, pltpu.roll(x, 2 * j + 1, axis=1), accs[v]))
        return tuple(out)

    inter = lax.fori_loop(0, 64, pack_ocean, tuple(jnp.zeros((8, LANES), F32) for _ in range(8)))
    even = (lane8 & 1) == 0
    for v in range(4):
        p0, p1 = inter[2 * v], inter[2 * v + 1]
        opack[0, v] = jnp.where(even, p0, pltpu.roll(p1, 1, axis=1))
        opack[1, v] = jnp.where(even, pltpu.roll(p0, LANES - 1, axis=1), p1)

    pl.semaphore_wait(barrier, NW - 1 + 6)

    near = []

    def send(src, dst, device):
        k = len(near)
        copy = pltpu.make_async_remote_copy(
            src_ref=src,
            dst_ref=dst,
            send_sem=near_send.at[k],
            recv_sem=near_recv.at[k],
            device_id=device,
            device_id_type=MESH,
        )
        copy.start()
        near.append(copy)
        return copy

    east = lambda dw: {"wide": wide_of[dw], "narrow": np_}
    west = lambda dw: {"wide": wide_of[dw], "narrow": nm}
    south = {"wide": wp, "narrow": n}
    north = {"wide": wm, "narrow": n}

    edges = []
    for dw in (0, 1, -1):
        edges.append(send(msg.at[0], msg_recv.at[1 - dw], east(dw)))
        edges.append(send(msg.at[1], msg_recv.at[3 + 1 - dw], west(dw)))

    def exchange(src, dst, send_sems, recv_sems):
        def one(i, carry):
            d = lax.rem(w + i, NW)
            pltpu.make_async_remote_copy(
                src_ref=src.at[d],
                dst_ref=dst.at[w],
                send_sem=send_sems.at[d],
                recv_sem=recv_sems.at[w],
                device_id={"wide": d, "narrow": n},
                device_id_type=MESH,
            ).start()
            return carry

        lax.fori_loop(1, NW, one, 0)

    def settle(src, dst, send_sems, recv_sems, sending):
        def one(i, carry):
            d = lax.rem(w + i, NW)
            copy = pltpu.make_async_remote_copy(
                src_ref=src.at[d],
                dst_ref=dst.at[d],
                send_sem=send_sems.at[d],
                recv_sem=recv_sems.at[d],
                device_id={"wide": d, "narrow": n},
                device_id_type=MESH,
            )
            if sending:
                copy.wait_send()
            else:
                copy.wait_recv()
            return carry

        lax.fori_loop(1, NW, one, 0)

    ocean_rows = []
    ocean_rows.append(send(oces[2].at[pl.ds(150, 10)], oc.at[pl.ds(360, 10)], south))
    ocean_rows.append(send(oces[2].at[pl.ds(0, 10)], oc.at[pl.ds(360 + 170, 10)], north))
    mask_rows = []
    for j, ref in ((0, ground_ref), (1, wet_ref)):
        mask_rows.append(send(ref.at[pl.ds(8, 8)], gw_recv.at[2 * j], south))
        mask_rows.append(send(ref.at[pl.ds(0, 8)], gw_recv.at[2 * j + 1], north))
    exchange(table, arrived, a2a_send, a2a_recv)
    ice_rows = []
    for f in range(3):
        ice_rows.append(send(ices[f].at[:, pl.ds(8, 8), :], rowbuf.at[f], south))
        ice_rows.append(send(ices[f].at[:, pl.ds(0, 8), :], rowbuf.at[3 + f], north))
    for f in range(2):
        ocean_rows.append(send(oces[f].at[pl.ds(150, 10)], oc.at[pl.ds(f * 180, 10)], south))
        ocean_rows.append(send(oces[f].at[pl.ds(0, 10)], oc.at[pl.ds(f * 180 + 170, 10)], north))

    ring_row = iota((RING, WIDTH), 0)
    ring_col = iota((RING, WIDTH), 1)
    global_row = w * ROWS + jnp.where(ring_row < 20, ring_row, ring_row - RING)
    global_col = n * LANES + jnp.where(ring_col < 192, ring_col, ring_col - WIDTH)
    good = (global_row >= 0) & (global_row < NW * ROWS) & (global_col >= 0) & (global_col < NN * LANES)
    inside = jnp.where(good, 1.0, 0.0)

    for load in loads[3:]:
        load.wait()
    for copy in ice_rows:
        copy.wait_recv()
    sub8 = iota((8, LANES), 0)
    edge_in = inside[16:24, 0:LANES]
    for f in range(3):
        def stitch(l, carry, f=f):
            merged = jnp.where(sub8 < 4, rowbuf[3 + f, l], rowbuf[f, l])
            E[f * LAYERS + l, pl.ds(16, 8), pl.ds(0, LANES)] = merged * edge_in
            return carry

        lax.fori_loop(0, LAYERS, stitch, 0)

    def pack_ice(j, accs):
        out = []
        for v in range(6):
            k = v * 16 + j
            if v == 5:
                k = jnp.minimum(k, 89)
            x = E[k // 3, pl.ds(pl.multiple_of(8 * (k % 3), 8), 8), pl.ds(0, LANES)]
            out.append(jnp.where((lane8 >> 3) == j, pltpu.roll(x, 8 * j + 4, axis=1), accs[v]))
        return tuple(out)

    inter = lax.fori_loop(0, 16, pack_ice, tuple(jnp.zeros((8, LANES), F32) for _ in range(6)))
    low = (lane8 & 7) < 4
    for v in range(3):
        p0, p1 = inter[2 * v], inter[2 * v + 1]
        ipack[0, v] = jnp.where(low, p0, pltpu.roll(p1, 4, axis=1))
        ipack[1, v] = jnp.where(low, pltpu.roll(p0, LANES - 4, axis=1), p1)
    ice_cols = [send(ipack.at[0], irecv.at[0], east(0)), send(ipack.at[1], irecv.at[1], west(0))]
    ocean_cols = [send(opack.at[0], orecv.at[0], east(0)), send(opack.at[1], orecv.at[1], west(0))]

    for copy in mask_rows + ocean_rows[:2] + edges:
        copy.wait_recv()
    g_below, g_above = gw_recv[1].astype(F32), gw_recv[0].astype(F32)
    w_below, w_above = gw_recv[3].astype(F32), gw_recv[2].astype(F32)
    left_msgs = (msg_recv[1], msg_recv[2], msg_recv[0])
    right_msgs = (msg_recv[4], msg_recv[5], msg_recv[3])

    row16 = iota((ROWS, LANES), 0)
    lane16 = iota((ROWS, LANES), 1)
    has_n = jnp.where(w > 0, 1.0, 0.0)
    has_s = jnp.where(w < NW - 1, 1.0, 0.0)
    has_w = jnp.where(n > 0, 1.0, 0.0)
    has_e = jnp.where(n < NN - 1, 1.0, 0.0)

    def four(x, first, last, west_col, east_col):
        north_x = jnp.where(row16 == 0, jnp.broadcast_to(first, (ROWS, LANES)), up(x))
        south_x = jnp.where(row16 == 15, jnp.broadcast_to(last, (ROWS, LANES)), down(x))
        west_x = jnp.where(lane16 == 0, west_col, left_of(x))
        east_x = jnp.where(lane16 == 127, east_col, right_of(x))
        return north_x, south_x, west_x, east_x

    wet_four = four(
        wet,
        w_above[7:8, :] * has_n,
        w_below[0:1, :] * has_s,
        unpack_col(left_msgs[0], 1) * has_w,
        unpack_col(right_msgs[0], 1) * has_e,
    )
    t_four = four(
        t0,
        oc[360, 0:1, :],
        oc[360 + 170, 0:1, :],
        unpack_col(left_msgs[0], 0),
        unpack_col(right_msgs[0], 0),
    )
    t_mixed = t0
    for i in range(4):
        weight = 0.2 * (wet * wet_four[i])
        weights[i] = weight
        t_mixed = t_mixed + weight * (t_four[i] - t0)

    settle(table, arrived, a2a_send, a2a_recv, False)
    linked = jnp.concatenate(
        [jnp.where(jnp.full((1, LANES), ocean_links[q], jnp.int32) >= 0, 1.0, 0.0) for q in range(ROWS)],
        axis=0,
    )
    ocean_draft = gather(arrived, ocean_links)
    melt = 0.5 * (t_mixed - (0.0832 - 0.761 * ocean_draft)) * wet * linked
    build_table(table2, melt, ocean_links)
    arrived2[w] = table2[w]
    exchange(table2, arrived2, a2a_send2, a2a_recv2)
    melt_out[...] = melt

    ground24 = ring_field(
        grounded,
        g_below,
        g_above,
        *[
            tuple(pltpu.roll(m, LANES - 32, axis=1) for m in msgs)
            for msgs in (left_msgs, right_msgs)
        ],
    )
    friction = 0.1 + 9.9 * ground24

    for copy in ice_cols:
        copy.wait_recv()
    for v in range(3):
        r, l = irecv[0, v], irecv[1, v]
        iquilt[2 * v] = jnp.where(low, r, pltpu.roll(l, 4, axis=1))
        iquilt[2 * v + 1] = jnp.where(low, pltpu.roll(r, LANES - 4, axis=1), l)
    rim_in = inside[:, LANES:]

    def unpack_ice(fl, carry):
        for g in range(3):
            k = fl * 3 + g
            j = k % 16
            x = pltpu.roll(iquilt[k // 16], LANES - 4 - 8 * j, axis=1)
            E[fl, pl.ds(8 * g, 8), pl.ds(LANES, LANES)] = x * rim_in[8 * g : 8 * g + 8, :]
        return carry

    lax.fori_loop(0, 30, unpack_ice, 0)

    def first_sweep(l, carry):
        lu, ld = jnp.minimum(l + 1, LAYERS - 1), jnp.maximum(l - 1, 0)
        is_last = jnp.where(l == LAYERS - 1, 1.0, 0.0)
        is_first = jnp.where(l == 0, 1.0, 0.0)
        sx, sy, diag, _ = sweep(
            (E[l], E[LAYERS + l]),
            ((E[lu], E[LAYERS + lu]), (E[ld], E[LAYERS + ld])),
            E[2 * LAYERS + l],
            is_last,
            is_first,
            inside,
            friction,
            RING,
            WIDTH,
        )
        SX[l] = sx
        SY[l] = sy
        RD[l] = inside / diag
        return carry

    lax.fori_loop(0, LAYERS, first_sweep, 0)

    settle(table2, arrived2, a2a_send2, a2a_recv2, False)
    ice_melt = gather(arrived2, ice_links)
    new_thick = thick - 0.05 * ice_melt * (1.0 - grounded)
    thick_out[...] = new_thick
    msg3[0] = pack_cols([(new_thick, 125), (new_thick, 126), (new_thick, 127)])
    msg3[1] = pack_cols([(new_thick, 0), (new_thick, 1), (new_thick, 2)])
    thick_edges = []
    for dw in (0, 1, -1):
        thick_edges.append(send(msg3.at[0], msg3_recv.at[1 - dw], east(dw)))
        thick_edges.append(send(msg3.at[1], msg3_recv.at[3 + 1 - dw], west(dw)))
    thick_edges.append(send(thick_out.at[pl.ds(8, 8)], t_recv.at[0], south))
    thick_edges.append(send(thick_out.at[pl.ds(0, 8)], t_recv.at[1], north))

    for copy in ocean_cols + ocean_rows[2:]:
        copy.wait_recv()
    for v in range(4):
        r, l = orecv[0, v], orecv[1, v]
        quilt[2 * v] = jnp.where(even, l, pltpu.roll(r, 1, axis=1))
        quilt[2 * v + 1] = jnp.where(even, pltpu.roll(l, LANES - 1, axis=1), r)
    at_first = lane8 == 0
    at_last = lane8 == 127

    def mix_row(r, carry):
        weight = [jnp.broadcast_to(weights[i, pl.ds(r, 1), :], (8, LANES)) for i in range(4)]
        for f in range(3):
            for g in range(GROUPS):
                k = f * 160 + r * 10 + g
                at = f * 180 + 10 + r * 10 + g
                j = k % 64
                edge = pltpu.roll(quilt[k // 64], LANES - 1 - 2 * j, axis=1)
                x = oc[at]
                x_w = jnp.where(at_first, edge, pltpu.roll(x, 1, axis=1))
                x_e = jnp.where(at_last, edge, pltpu.roll(x, LANES - 1, axis=1))
                out = x + weight[0] * (oc[at - 10] - x)
                out = out + weight[1] * (oc[at + 10] - x)
                out = out + weight[2] * (x_w - x)
                out = out + weight[3] * (x_e - x)
                if f == 2 and g == 0:
                    lower = jnp.broadcast_to(melt_out[pl.ds(r, 1), :], (8, LANES))
                    out = jnp.where(sub8 == 0, out - 0.2 * lower, out)
                ocean_out[f, r * 10 + g] = out
        return carry

    lax.fori_loop(0, ROWS, mix_row, 0)

    for copy in thick_edges:
        copy.wait_recv()
    thick24 = ring_field(
        new_thick,
        t_recv[1],
        t_recv[0],
        (msg3_recv[1], msg3_recv[2], msg3_recv[0]),
        (msg3_recv[4], msg3_recv[5], msg3_recv[3]),
    )
    surface = thick24 * (0.1 + 0.9 * ground24) * inside
    stress_x = -0.05 * thick24 * (down(surface) - up(surface))
    stress_y = -0.05 * thick24 * (right_of(surface) - left_of(surface))

    def finish_first(l, carry):
        rd = RD[l]
        SX[l] = (SX[l] + stress_x) * rd
        SY[l] = (SY[l] + stress_y) * rd
        return carry

    lax.fori_loop(0, LAYERS, finish_first, 0)
    friction16 = friction[:ROWS, :LANES]
    stress_x16 = stress_x[:ROWS, :LANES]
    stress_y16 = stress_y[:ROWS, :LANES]

    def second_sweep(l, carry):
        lu, ld = jnp.minimum(l + 1, LAYERS - 1), jnp.maximum(l - 1, 0)
        is_last = jnp.where(l == LAYERS - 1, 1.0, 0.0)
        is_first = jnp.where(l == 0, 1.0, 0.0)
        heat = E[2 * LAYERS + l]
        sx, sy, diag, work = sweep(
            (SX[l], SY[l]),
            ((SX[lu], SY[lu]), (SX[ld], SY[ld])),
            heat,
            is_last,
            is_first,
            inside,
            friction16,
            ROWS,
            LANES,
        )
        inv = 1.0 / diag
        ice_out[0, l] = (sx + stress_x16) * inv
        ice_out[1, l] = (sy + stress_y16) * inv
        ice_out[2, l] = heat[:ROWS, :LANES] + 0.01 * work
        return carry

    lax.fori_loop(0, LAYERS, second_sweep, 0)

    for copy in near:
        copy.wait_send()
    settle(table, arrived, a2a_send, a2a_recv, True)
    settle(table2, arrived2, a2a_send2, a2a_recv2, True)


def local(
    NW,
    NN,
    ice_x,
    ice_y,
    ice_temp,
    ocean_x,
    ocean_y,
    ocean_temp,
    thick,
    grounded_mask,
    wet_mask,
    ice_links,
    ocean_links,
):
    anywhere = pl.BlockSpec(memory_space=pl.ANY)
    vmem = pl.BlockSpec(memory_space=pltpu.VMEM)
    smem = pl.BlockSpec(memory_space=pltpu.SMEM)
    ices = [jnp.transpose(x, (1, 0, 2)) for x in (ice_x, ice_y, ice_temp)]
    oces = [x.reshape(160, 8, LANES) for x in (ocean_x, ocean_y, ocean_temp)]
    V = lambda *shape: pltpu.VMEM(shape, F32)
    D = pltpu.SemaphoreType.DMA
    ice, ocean, new_thick, melt = pl.pallas_call(
        functools.partial(kernel, NW, NN),
        out_shape=(
            jax.ShapeDtypeStruct((3, LAYERS, ROWS, LANES), F32),
            jax.ShapeDtypeStruct((3, 160, 8, LANES), F32),
            jax.ShapeDtypeStruct((ROWS, LANES), F32),
            jax.ShapeDtypeStruct((ROWS, LANES), F32),
        ),
        in_specs=[anywhere] * 6 + [vmem] * 3 + [smem] * 2,
        out_specs=[vmem] * 4,
        scratch_shapes=[
            V(30, RING, WIDTH),
            V(6, LAYERS, 8, LANES),
            V(540, 8, LANES),
            V(2, 3, 8, LANES),
            V(2, 3, 8, LANES),
            V(2, 4, 8, LANES),
            V(2, 4, 8, LANES),
            V(8, 8, LANES),
            V(6, 8, LANES),
            V(2, 1, LANES),
            V(6, 1, LANES),
            V(2, 1, LANES),
            V(6, 1, LANES),
            pltpu.VMEM((4, 8, LANES), jnp.int32),
            V(2, 8, LANES),
            V(NW, 1, LANES),
            V(NW, 1, LANES),
            V(NW, 1, LANES),
            V(NW, 1, LANES),
            V(4, ROWS, LANES),
            V(LAYERS, RING, WIDTH),
            V(LAYERS, RING, WIDTH),
            V(LAYERS, RING, WIDTH),
            D((6,)),
            D((40,)),
            D((40,)),
            D((NW,)),
            D((NW,)),
            D((NW,)),
            D((NW,)),
        ],
        compiler_params=pltpu.CompilerParams(collective_id=0, has_side_effects=True),
    )(
        *ices,
        *oces,
        thick,
        grounded_mask,
        wet_mask,
        ice_links.reshape(ROWS),
        ocean_links.reshape(ROWS),
    )
    return (
        jnp.transpose(ice, (0, 2, 1, 3)),
        ocean.reshape(3, ROWS, 80, LANES),
        new_thick,
        melt,
    )


def solution(mesh):
    deep = P("wide", None, "narrow")
    flat = P("wide", "narrow")
    return jax.shard_map(
        functools.partial(local, mesh.shape["wide"], mesh.shape["narrow"]),
        mesh=mesh,
        in_specs=(deep,) * 6 + (flat,) * 5,
        out_specs=(P(None, "wide", None, "narrow"), P(None, "wide", None, "narrow"), flat, flat),
        check_vma=False,
    )
```

```python
import functools

import jax
import jax.numpy as jnp
from jax import lax
from jax.experimental import pallas as pl
from jax.experimental.pallas import tpu as pltpu
from jax.sharding import PartitionSpec as P

MESH = pl.DeviceIdType.MESH
F32 = jnp.float32

ROWS = 16
LANES = 128
LAYERS = 10
GROUPS = 10
RING = 24
WIDTH = 256


def iota(shape, dim):
    return lax.broadcasted_iota(jnp.int32, shape, dim)


def pack_cols(pieces):
    lane = iota((ROWS, LANES), 1)
    row = iota((ROWS, LANES), 0)
    acc = jnp.zeros((ROWS, LANES), F32)
    for j, (value, col) in enumerate(pieces):
        wide = jnp.broadcast_to(value[:, col : col + 1], (ROWS, LANES))
        acc = jnp.where(lane == row + 16 * j, wide, acc)
    return jnp.sum(acc, axis=0, keepdims=True)


def unpack_col(mid, j):
    lane = iota((ROWS, LANES), 1)
    row = iota((ROWS, LANES), 0)
    wide = jnp.broadcast_to(mid, (ROWS, LANES))
    return jnp.sum(jnp.where(lane == row + 16 * j, wide, 0.0), axis=1, keepdims=True)


def unpack_rim(mid, below, above, j):
    lane = iota((8, LANES), 1)
    sub = iota((8, LANES), 0)
    edge = jnp.where(sub < 4, jnp.broadcast_to(below, (8, LANES)), jnp.broadcast_to(above, (8, LANES)))
    place = jnp.where(sub < 4, sub, sub + 8)
    outer = jnp.sum(jnp.where(lane == place + 16 * j, edge, 0.0), axis=1, keepdims=True)
    return jnp.concatenate([unpack_col(mid, j), outer], axis=0)


def ring_field(own, below, above, left, right):
    sub = iota((8, LANES), 0)
    main = jnp.concatenate([own, jnp.where(sub < 4, below, above)], axis=0)
    lane = iota((RING, LANES), 1)
    rim = jnp.zeros((RING, LANES), F32)
    for j in range(3):
        rim = jnp.where(lane == 125 + j, unpack_rim(*left, j), rim)
        rim = jnp.where(lane == j, unpack_rim(*right, j), rim)
    return jnp.concatenate([main, rim], axis=1)


def up(x):
    return pltpu.roll(x, 1, axis=0)


def down(x):
    return pltpu.roll(x, x.shape[0] - 1, axis=0)


def left_of(x):
    return pltpu.roll(x, 1, axis=1)


def right_of(x):
    return pltpu.roll(x, x.shape[1] - 1, axis=1)


def sweep(here, above, heat, is_last, is_first, inside, friction, rows, width):
    a, b = here
    has_above = 1.0 - is_last
    has_below = 1.0 - is_first
    (au, bu), (ad, bd) = above
    aN, aS, aW, aE = up(a), down(a), left_of(a), right_of(a)
    bN, bS, bW, bE = up(b), down(b), left_of(b), right_of(b)
    ux, uy = 0.5 * (aS - aN), 0.5 * (aE - aW)
    vx, vy = 0.5 * (bS - bN), 0.5 * (bE - bW)
    uz, vz = au - a, bu - b
    shear = uy + vx
    eps2 = ux * ux + vy * vy + ux * vy + 0.25 * (shear * shear) + 0.25 * (uz * uz + vz * vz)
    eta = jnp.exp(0.25 * heat - jnp.log(eps2 + 0.01) * (1.0 / 3.0)) * inside
    cut = lambda x: x[:rows, :width]
    c = cut(eta)
    diag = c * (has_above + has_below) + friction
    up_c, down_c = c * has_above, c * has_below
    sx = up_c * cut(au) + down_c * cut(ad)
    sy = up_c * cut(bu) + down_c * cut(bd)
    for e, x, y in (
        (up(eta), aN, bN),
        (down(eta), aS, bS),
        (left_of(eta), aW, bW),
        (right_of(eta), aE, bE),
    ):
        face = 0.5 * (c + cut(e))
        diag = diag + face
        sx = sx + face * cut(x)
        sy = sy + face * cut(y)
    return sx, sy, diag, c * cut(eps2)


def kernel(
    NW,
    NN,
    ice_x,
    ice_y,
    ice_t,
    oce_x,
    oce_y,
    oce_t,
    thick_in,
    ground_in,
    wet_in,
    ice_links_in,
    ocean_links_in,
    ice_out,
    ocean_out,
    thick_out,
    melt_out,
    thick_ref,
    ground_ref,
    wet_ref,
    ice_links,
    ocean_links,
    E,
    rowbuf,
    oc,
    ipack,
    irecv,
    opack,
    orecv,
    quilt,
    iquilt,
    msg,
    msg_recv,
    msg3,
    msg3_recv,
    gw_recv,
    t_recv,
    table,
    arrived,
    table2,
    arrived2,
    weights,
    SX,
    SY,
    RD,
    local_sem,
    near_send,
    near_recv,
    a2a_send,
    a2a_recv,
    a2a_send2,
    a2a_recv2,
):
    w = lax.axis_index("wide")
    n = lax.axis_index("narrow")
    wp, wm = lax.rem(w + 1, NW), lax.rem(w + NW - 1, NW)
    np_, nm = lax.rem(n + 1, NN), lax.rem(n + NN - 1, NN)
    wide_of = {-1: wm, 0: w, 1: wp}
    ices = (ice_x, ice_y, ice_t)
    oces = (oce_x, oce_y, oce_t)

    barrier = pltpu.get_barrier_semaphore()

    def greet(i, carry):
        pl.semaphore_signal(
            barrier, 1, device_id={"wide": lax.rem(w + i, NW), "narrow": n}, device_id_type=MESH
        )
        return carry

    has_n, has_s, has_w, has_e = w > 0, w < NW - 1, n > 0, n < NN - 1
    row_ok = {-1: has_n, 0: None, 1: has_s}

    def both(x, y):
        return x if y is None else x & y

    greeted = jnp.int32(NW - 1)
    for nb, ok in ((nm, has_w), (np_, has_e)):
        for dw in (0, -1, 1):
            here = both(ok, row_ok[dw])

            @pl.when(here)
            def _(dw=dw, nb=nb):
                pl.semaphore_signal(
                    barrier, 1, device_id={"wide": wide_of[dw], "narrow": nb}, device_id_type=MESH
                )

            greeted = greeted + jnp.where(here, 1, 0)
    lax.fori_loop(1, NW, greet, 0)

    loads = []
    for f in range(3):
        loads.append(pltpu.make_async_copy(oces[f], oc.at[pl.ds(f * 180 + 10, 160)], local_sem.at[f]))
    for f in range(3):
        loads.append(
            pltpu.make_async_copy(
                ices[f],
                E.at[pl.ds(f * LAYERS, LAYERS), pl.ds(0, ROWS), pl.ds(0, LANES)],
                local_sem.at[3 + f],
            )
        )
    small = []
    for i, (src, dst) in enumerate(
        (
            (thick_in, thick_ref),
            (ground_in, ground_ref),
            (wet_in, wet_ref),
            (ice_links_in, ice_links),
            (ocean_links_in, ocean_links),
        )
    ):
        small.append(pltpu.make_async_copy(src, dst, local_sem.at[6 + i]))
    for load in small + [loads[2], loads[0], loads[1]] + loads[3:]:
        load.start()

    def blank(ref, start, count):
        ref[pl.ds(start, count)] = jnp.zeros((count,) + ref.shape[1:], ref.dtype)

    for side, ok in ((0, has_w), (1, has_e)):

        @pl.when(jnp.logical_not(ok))
        def _(side=side):
            blank(msg_recv, 3 * side, 3)
            blank(msg3_recv, 3 * side, 3)
            blank(orecv, side, 1)
            blank(irecv, side, 1)

    for side, ok in ((0, has_n), (1, has_s)):

        @pl.when(jnp.logical_not(ok))
        def _(side=side):
            for f in range(3):
                blank(oc, f * 180 + 170 * side, 10)
            blank(rowbuf, 3 * side, 3)
            blank(gw_recv, side, 1)
            blank(gw_recv, 2 + side, 1)
            blank(t_recv, side, 1)
            for k in (0, 3):
                blank(msg_recv, k + 2 * side, 1)
                blank(msg3_recv, k + 2 * side, 1)

    for load in small:
        load.wait()

    grounded = ground_ref[...].astype(F32)
    wet = wet_ref[...].astype(F32)
    thick = thick_ref[...]
    draft = 0.9 * thick * (1.0 - grounded)

    def build_table(dst, at, values, links):
        dest = iota((NW, LANES), 0)
        acc = jnp.zeros((NW, LANES), F32)
        for q in range(ROWS):
            hit = dest == (links[q] >> 4)
            acc = jnp.where(hit, jnp.broadcast_to(values[q : q + 1, :], (NW, LANES)), acc)
        dst[:, :, pl.ds(at, LANES)] = acc.reshape(NW, 1, LANES)

    def gather(src, at, links):
        rows = []
        for q in range(ROWS):
            link = links[q]
            row = src[jnp.maximum(link, 0) >> 4, :, pl.ds(at, LANES)]
            rows.append(jnp.where(jnp.full((1, LANES), link, jnp.int32) >= 0, row, 0.0))
        return jnp.concatenate(rows, axis=0)

    build_table(table, 0, draft, ice_links)
    build_table(table, LANES, wet, ocean_links)
    arrived[w] = table[w]

    loads[2].wait()
    t0 = jnp.concatenate([oc[360 + 10 + 10 * r, 0:1, :] for r in range(ROWS)], axis=0)
    msg[0] = pack_cols([(t0, 127), (wet, 127), (grounded, 125), (grounded, 126), (grounded, 127)])
    msg[1] = pack_cols([(t0, 0), (wet, 0), (grounded, 0), (grounded, 1), (grounded, 2)])

    lane8 = iota((8, LANES), 1)
    for load in loads[:2]:
        load.wait()

    def pack_ocean(j, accs):
        out = []
        for v in range(8):
            k = v * 64 + j
            if v == 7:
                k = jnp.minimum(k, 479)
            x = oc[k + 20 * (k // 160) + 10]
            out.append(jnp.where((lane8 >> 1) == j, pltpu.roll(x, 2 * j + 1, axis=1), accs[v]))
        return tuple(out)

    inter = lax.fori_loop(0, 64, pack_ocean, tuple(jnp.zeros((8, LANES), F32) for _ in range(8)))
    even = (lane8 & 1) == 0
    for v in range(4):
        p0, p1 = inter[2 * v], inter[2 * v + 1]
        opack[0, v] = jnp.where(even, p0, pltpu.roll(p1, 1, axis=1))
        opack[1, v] = jnp.where(even, pltpu.roll(p0, LANES - 1, axis=1), p1)

    pl.semaphore_wait(barrier, greeted)

    near = []

    def send(src, dst, device, goes, comes):
        k = len(near)
        copy = pltpu.make_async_remote_copy(
            src_ref=src,
            dst_ref=dst,
            send_sem=near_send.at[k],
            recv_sem=near_recv.at[k],
            device_id=device,
            device_id_type=MESH,
        )
        pl.when(goes)(lambda: copy.start())
        near.append((copy, goes))
        return copy, comes

    def receive(copies):
        for copy, comes in copies:
            pl.when(comes)(lambda copy=copy: copy.wait_recv())

    def east(dw):
        device = {"wide": wide_of[dw], "narrow": np_}
        return device, both(has_e, row_ok[dw]), both(has_w, row_ok[-dw])

    def west(dw):
        device = {"wide": wide_of[dw], "narrow": nm}
        return device, both(has_w, row_ok[dw]), both(has_e, row_ok[-dw])

    south = {"wide": wp, "narrow": n}, has_s, has_n
    north = {"wide": wm, "narrow": n}, has_n, has_s

    edges = []
    for dw in (0, 1, -1):
        edges.append(send(msg.at[0], msg_recv.at[1 - dw], *east(dw)))
        edges.append(send(msg.at[1], msg_recv.at[3 + 1 - dw], *west(dw)))

    def exchange(src, dst, send_sems, recv_sems):
        def one(i, carry):
            d = lax.rem(w + i, NW)
            pltpu.make_async_remote_copy(
                src_ref=src.at[d],
                dst_ref=dst.at[w],
                send_sem=send_sems.at[d],
                recv_sem=recv_sems.at[w],
                device_id={"wide": d, "narrow": n},
                device_id_type=MESH,
            ).start()
            return carry

        lax.fori_loop(1, NW, one, 0)

    def settle(src, dst, send_sems, recv_sems, sending):
        def one(i, carry):
            d = lax.rem(w + i, NW)
            copy = pltpu.make_async_remote_copy(
                src_ref=src.at[d],
                dst_ref=dst.at[d],
                send_sem=send_sems.at[d],
                recv_sem=recv_sems.at[d],
                device_id={"wide": d, "narrow": n},
                device_id_type=MESH,
            )
            if sending:
                copy.wait_send()
            else:
                copy.wait_recv()
            return carry

        lax.fori_loop(1, NW, one, 0)

    ocean_rows = []
    ocean_rows.append(send(oces[2].at[pl.ds(150, 10)], oc.at[pl.ds(360, 10)], *south))
    ocean_rows.append(send(oces[2].at[pl.ds(0, 10)], oc.at[pl.ds(360 + 170, 10)], *north))
    mask_rows = []
    for j, ref in ((0, ground_ref), (1, wet_ref)):
        mask_rows.append(send(ref.at[pl.ds(8, 8)], gw_recv.at[2 * j], *south))
        mask_rows.append(send(ref.at[pl.ds(0, 8)], gw_recv.at[2 * j + 1], *north))
    ice_rows = []
    for f in range(3):
        ice_rows.append(send(ices[f].at[:, pl.ds(8, 8), :], rowbuf.at[f], *south))
        ice_rows.append(send(ices[f].at[:, pl.ds(0, 8), :], rowbuf.at[3 + f], *north))
    exchange(table, arrived, a2a_send, a2a_recv)
    for f in range(2):
        ocean_rows.append(send(oces[f].at[pl.ds(150, 10)], oc.at[pl.ds(f * 180, 10)], *south))
        ocean_rows.append(send(oces[f].at[pl.ds(0, 10)], oc.at[pl.ds(f * 180 + 170, 10)], *north))

    ocean_cols = [send(opack.at[0], orecv.at[0], *east(0)), send(opack.at[1], orecv.at[1], *west(0))]

    ring_row = iota((RING, WIDTH), 0)
    ring_col = iota((RING, WIDTH), 1)
    global_row = w * ROWS + jnp.where(ring_row < 20, ring_row, ring_row - RING)
    global_col = n * LANES + jnp.where(ring_col < 192, ring_col, ring_col - WIDTH)
    good = (global_row >= 0) & (global_row < NW * ROWS) & (global_col >= 0) & (global_col < NN * LANES)
    inside = jnp.where(good, 1.0, 0.0)

    for load in loads[3:]:
        load.wait()
    receive(ice_rows)
    sub8 = iota((8, LANES), 0)
    edge_in = inside[16:24, 0:LANES]
    for f in range(3):
        def stitch(l, carry, f=f):
            merged = jnp.where(sub8 < 4, rowbuf[3 + f, l], rowbuf[f, l])
            E[f * LAYERS + l, pl.ds(16, 8), pl.ds(0, LANES)] = merged * edge_in
            return carry

        lax.fori_loop(0, LAYERS, stitch, 0)

    def pack_ice(j, accs):
        out = []
        for v in range(6):
            k = v * 16 + j
            if v == 5:
                k = jnp.minimum(k, 89)
            x = E[k // 3, pl.ds(pl.multiple_of(8 * (k % 3), 8), 8), pl.ds(0, LANES)]
            out.append(jnp.where((lane8 >> 3) == j, pltpu.roll(x, 8 * j + 4, axis=1), accs[v]))
        return tuple(out)

    inter = lax.fori_loop(0, 16, pack_ice, tuple(jnp.zeros((8, LANES), F32) for _ in range(6)))
    low = (lane8 & 7) < 4
    for v in range(3):
        p0, p1 = inter[2 * v], inter[2 * v + 1]
        ipack[0, v] = jnp.where(low, p0, pltpu.roll(p1, 4, axis=1))
        ipack[1, v] = jnp.where(low, pltpu.roll(p0, LANES - 4, axis=1), p1)
    ice_cols = [send(ipack.at[0], irecv.at[0], *east(0)), send(ipack.at[1], irecv.at[1], *west(0))]

    receive(mask_rows + ocean_rows[:2] + edges)
    g_below, g_above = gw_recv[1].astype(F32), gw_recv[0].astype(F32)
    w_below, w_above = gw_recv[3].astype(F32), gw_recv[2].astype(F32)
    left_msgs = (msg_recv[1], msg_recv[2], msg_recv[0])
    right_msgs = (msg_recv[4], msg_recv[5], msg_recv[3])

    row16 = iota((ROWS, LANES), 0)
    lane16 = iota((ROWS, LANES), 1)
    def four(x, first, last, west_col, east_col):
        north_x = jnp.where(row16 == 0, jnp.broadcast_to(first, (ROWS, LANES)), up(x))
        south_x = jnp.where(row16 == 15, jnp.broadcast_to(last, (ROWS, LANES)), down(x))
        west_x = jnp.where(lane16 == 0, west_col, left_of(x))
        east_x = jnp.where(lane16 == 127, east_col, right_of(x))
        return north_x, south_x, west_x, east_x

    wet_four = four(
        wet,
        w_above[7:8, :],
        w_below[0:1, :],
        unpack_col(left_msgs[0], 1),
        unpack_col(right_msgs[0], 1),
    )
    t_four = four(
        t0,
        oc[360, 0:1, :],
        oc[360 + 170, 0:1, :],
        unpack_col(left_msgs[0], 0),
        unpack_col(right_msgs[0], 0),
    )
    t_mixed = t0
    for i in range(4):
        weight = 0.2 * (wet * wet_four[i])
        weights[i] = weight
        t_mixed = t_mixed + weight * (t_four[i] - t0)

    build_table(table2, 0, t_mixed, ocean_links)
    arrived2[w] = table2[w]
    exchange(table2, arrived2, a2a_send2, a2a_recv2)

    def linked(links):
        return jnp.concatenate(
            [jnp.where(jnp.full((1, LANES), links[q], jnp.int32) >= 0, 1.0, 0.0) for q in range(ROWS)],
            axis=0,
        )

    settle(table, arrived, a2a_send, a2a_recv, False)
    ocean_draft = gather(arrived, 0, ocean_links)
    melt_out[...] = 0.5 * (t_mixed - (0.0832 - 0.761 * ocean_draft)) * wet * linked(ocean_links)
    ice_wet = gather(arrived, LANES, ice_links) * linked(ice_links)

    ground24 = ring_field(
        grounded,
        g_below,
        g_above,
        *[
            tuple(pltpu.roll(m, LANES - 32, axis=1) for m in msgs)
            for msgs in (left_msgs, right_msgs)
        ],
    )
    friction = 0.1 + 9.9 * ground24

    receive(ice_cols)
    for v in range(3):
        r, l = irecv[0, v], irecv[1, v]
        iquilt[2 * v] = jnp.where(low, r, pltpu.roll(l, 4, axis=1))
        iquilt[2 * v + 1] = jnp.where(low, pltpu.roll(r, LANES - 4, axis=1), l)
    rim_in = inside[:, LANES:]

    def unpack_ice(fl, carry):
        for g in range(3):
            k = fl * 3 + g
            j = k % 16
            x = pltpu.roll(iquilt[k // 16], LANES - 4 - 8 * j, axis=1)
            E[fl, pl.ds(8 * g, 8), pl.ds(LANES, LANES)] = x * rim_in[8 * g : 8 * g + 8, :]
        return carry

    lax.fori_loop(0, 30, unpack_ice, 0)

    def first_sweep(l, carry):
        lu, ld = jnp.minimum(l + 1, LAYERS - 1), jnp.maximum(l - 1, 0)
        is_last = jnp.where(l == LAYERS - 1, 1.0, 0.0)
        is_first = jnp.where(l == 0, 1.0, 0.0)
        sx, sy, diag, _ = sweep(
            (E[l], E[LAYERS + l]),
            ((E[lu], E[LAYERS + lu]), (E[ld], E[LAYERS + ld])),
            E[2 * LAYERS + l],
            is_last,
            is_first,
            inside,
            friction,
            RING,
            WIDTH,
        )
        SX[l] = sx
        SY[l] = sy
        RD[l] = inside / diag
        return carry

    lax.fori_loop(0, LAYERS, first_sweep, 0)

    receive(ocean_cols + ocean_rows[2:])
    for v in range(4):
        r, l = orecv[0, v], orecv[1, v]
        quilt[2 * v] = jnp.where(even, l, pltpu.roll(r, 1, axis=1))
        quilt[2 * v + 1] = jnp.where(even, pltpu.roll(l, LANES - 1, axis=1), r)
    at_first = lane8 == 0
    at_last = lane8 == 127

    def mix_row(r, carry):
        weight = [jnp.broadcast_to(weights[i, pl.ds(r, 1), :], (8, LANES)) for i in range(4)]
        for f in range(3):
            for g in range(GROUPS):
                k = f * 160 + r * 10 + g
                at = f * 180 + 10 + r * 10 + g
                j = k % 64
                edge = pltpu.roll(quilt[k // 64], LANES - 1 - 2 * j, axis=1)
                x = oc[at]
                x_w = jnp.where(at_first, edge, pltpu.roll(x, 1, axis=1))
                x_e = jnp.where(at_last, edge, pltpu.roll(x, LANES - 1, axis=1))
                out = x + weight[0] * (oc[at - 10] - x)
                out = out + weight[1] * (oc[at + 10] - x)
                out = out + weight[2] * (x_w - x)
                out = out + weight[3] * (x_e - x)
                if f == 2 and g == 0:
                    lower = jnp.broadcast_to(melt_out[pl.ds(r, 1), :], (8, LANES))
                    out = jnp.where(sub8 == 0, out - 0.2 * lower, out)
                ocean_out[f, r * 10 + g] = out
        return carry

    lax.fori_loop(0, 7, mix_row, 0)

    settle(table2, arrived2, a2a_send2, a2a_recv2, False)
    ice_melt = 0.5 * (gather(arrived2, 0, ice_links) - (0.0832 - 0.761 * draft)) * ice_wet
    new_thick = thick - 0.05 * ice_melt * (1.0 - grounded)
    thick_out[...] = new_thick
    msg3[0] = pack_cols([(new_thick, 125), (new_thick, 126), (new_thick, 127)])
    msg3[1] = pack_cols([(new_thick, 0), (new_thick, 1), (new_thick, 2)])
    thick_edges = []
    for dw in (0, 1, -1):
        thick_edges.append(send(msg3.at[0], msg3_recv.at[1 - dw], *east(dw)))
        thick_edges.append(send(msg3.at[1], msg3_recv.at[3 + 1 - dw], *west(dw)))
    thick_edges.append(send(thick_out.at[pl.ds(8, 8)], t_recv.at[0], *south))
    thick_edges.append(send(thick_out.at[pl.ds(0, 8)], t_recv.at[1], *north))

    lax.fori_loop(7, ROWS, mix_row, 0)

    receive(thick_edges)
    thick24 = ring_field(
        new_thick,
        t_recv[1],
        t_recv[0],
        (msg3_recv[1], msg3_recv[2], msg3_recv[0]),
        (msg3_recv[4], msg3_recv[5], msg3_recv[3]),
    )
    surface = thick24 * (0.1 + 0.9 * ground24) * inside
    stress_x = -0.05 * thick24 * (down(surface) - up(surface))
    stress_y = -0.05 * thick24 * (right_of(surface) - left_of(surface))

    def finish_first(l, carry):
        rd = RD[l]
        SX[l] = (SX[l] + stress_x) * rd
        SY[l] = (SY[l] + stress_y) * rd
        return carry

    lax.fori_loop(0, LAYERS, finish_first, 0)
    friction16 = friction[:ROWS, :LANES]
    stress_x16 = stress_x[:ROWS, :LANES]
    stress_y16 = stress_y[:ROWS, :LANES]

    def second_sweep(l, carry):
        lu, ld = jnp.minimum(l + 1, LAYERS - 1), jnp.maximum(l - 1, 0)
        is_last = jnp.where(l == LAYERS - 1, 1.0, 0.0)
        is_first = jnp.where(l == 0, 1.0, 0.0)
        heat = E[2 * LAYERS + l]
        sx, sy, diag, work = sweep(
            (SX[l], SY[l]),
            ((SX[lu], SY[lu]), (SX[ld], SY[ld])),
            heat,
            is_last,
            is_first,
            inside,
            friction16,
            ROWS,
            LANES,
        )
        inv = 1.0 / diag
        ice_out[0, l] = (sx + stress_x16) * inv
        ice_out[1, l] = (sy + stress_y16) * inv
        ice_out[2, l] = heat[:ROWS, :LANES] + 0.01 * work
        return carry

    lax.fori_loop(0, LAYERS, second_sweep, 0)

    for copy, goes in near:
        pl.when(goes)(lambda copy=copy: copy.wait_send())
    settle(table, arrived, a2a_send, a2a_recv, True)
    settle(table2, arrived2, a2a_send2, a2a_recv2, True)


def writer(*refs):
    sources, targets, sems = refs[:4], refs[4:8], refs[8]
    copies = [pltpu.make_async_copy(sources[i], targets[i], sems.at[i]) for i in (1, 0, 2, 3)]
    for copy in copies:
        copy.start()
    for copy in copies:
        copy.wait()


def local(
    NW,
    NN,
    ice_x,
    ice_y,
    ice_temp,
    ocean_x,
    ocean_y,
    ocean_temp,
    thick,
    grounded_mask,
    wet_mask,
    ice_links,
    ocean_links,
):
    anywhere = pl.BlockSpec(memory_space=pl.ANY)
    vmem = pl.BlockSpec(memory_space=pltpu.VMEM)
    ices = [jnp.transpose(x, (1, 0, 2)) for x in (ice_x, ice_y, ice_temp)]
    oces = [x.reshape(160, 8, LANES) for x in (ocean_x, ocean_y, ocean_temp)]
    V = lambda *shape: pltpu.VMEM(shape, F32)
    D = pltpu.SemaphoreType.DMA
    shapes = ((3, LAYERS, ROWS, LANES), (3, 160, 8, LANES), (ROWS, LANES), (ROWS, LANES))
    results = pl.pallas_call(
        functools.partial(kernel, NW, NN),
        out_shape=[pltpu.VMEM(shape, F32) for shape in shapes],
        in_specs=[anywhere] * 11,
        out_specs=[vmem] * 4,
        scratch_shapes=[
            V(ROWS, LANES),
            pltpu.VMEM((ROWS, LANES), jnp.int32),
            pltpu.VMEM((ROWS, LANES), jnp.int32),
            pltpu.SMEM((ROWS,), jnp.int32),
            pltpu.SMEM((ROWS,), jnp.int32),
            V(30, RING, WIDTH),
            V(6, LAYERS, 8, LANES),
            V(540, 8, LANES),
            V(2, 3, 8, LANES),
            V(2, 3, 8, LANES),
            V(2, 4, 8, LANES),
            V(2, 4, 8, LANES),
            V(8, 8, LANES),
            V(6, 8, LANES),
            V(2, 1, LANES),
            V(6, 1, LANES),
            V(2, 1, LANES),
            V(6, 1, LANES),
            pltpu.VMEM((4, 8, LANES), jnp.int32),
            V(2, 8, LANES),
            V(NW, 1, 2 * LANES),
            V(NW, 1, 2 * LANES),
            V(NW, 1, LANES),
            V(NW, 1, LANES),
            V(4, ROWS, LANES),
            V(LAYERS, RING, WIDTH),
            V(LAYERS, RING, WIDTH),
            V(LAYERS, RING, WIDTH),
            D((11,)),
            D((40,)),
            D((40,)),
            D((NW,)),
            D((NW,)),
            D((NW,)),
            D((NW,)),
        ],
        compiler_params=pltpu.CompilerParams(collective_id=0, has_side_effects=True),
    )(
        *ices,
        *oces,
        thick,
        grounded_mask,
        wet_mask,
        ice_links.reshape(ROWS),
        ocean_links.reshape(ROWS),
    )
    ice, ocean, new_thick, melt = pl.pallas_call(
        writer,
        out_shape=[jax.ShapeDtypeStruct(shape, F32) for shape in shapes],
        in_specs=[vmem] * 4,
        out_specs=[anywhere] * 4,
        scratch_shapes=[D((4,))],
    )(*[pltpu.with_memory_space_constraint(x, pltpu.VMEM) for x in results])
    return (
        jnp.transpose(ice, (0, 2, 1, 3)),
        ocean.reshape(3, ROWS, 80, LANES),
        new_thick,
        melt,
    )


def solution(mesh):
    deep = P("wide", None, "narrow")
    flat = P("wide", "narrow")
    return jax.shard_map(
        functools.partial(local, mesh.shape["wide"], mesh.shape["narrow"]),
        mesh=mesh,
        in_specs=(deep,) * 6 + (flat,) * 5,
        out_specs=(P(None, "wide", None, "narrow"), P(None, "wide", None, "narrow"), flat, flat),
        check_vma=False,
    )
```

```python
import functools

import jax
import jax.numpy as jnp
from jax import lax
from jax.experimental import pallas as pl
from jax.experimental.pallas import tpu as pltpu
from jax.sharding import PartitionSpec as P

MESH = pl.DeviceIdType.MESH
F32 = jnp.float32

ROWS = 16
LANES = 128
LAYERS = 10
GROUPS = 10
RING = 24
WIDTH = 256


def iota(shape, dim):
    return lax.broadcasted_iota(jnp.int32, shape, dim)


def pack_cols(pieces):
    lane = iota((ROWS, LANES), 1)
    row = iota((ROWS, LANES), 0)
    acc = jnp.zeros((ROWS, LANES), F32)
    for j, (value, col) in enumerate(pieces):
        wide = jnp.broadcast_to(value[:, col : col + 1], (ROWS, LANES))
        acc = jnp.where(lane == row + 16 * j, wide, acc)
    return jnp.sum(acc, axis=0, keepdims=True)


def unpack_col(mid, j):
    lane = iota((ROWS, LANES), 1)
    row = iota((ROWS, LANES), 0)
    wide = jnp.broadcast_to(mid, (ROWS, LANES))
    return jnp.sum(jnp.where(lane == row + 16 * j, wide, 0.0), axis=1, keepdims=True)


def unpack_rim(mid, below, above, j):
    lane = iota((8, LANES), 1)
    sub = iota((8, LANES), 0)
    edge = jnp.where(sub < 4, jnp.broadcast_to(below, (8, LANES)), jnp.broadcast_to(above, (8, LANES)))
    place = jnp.where(sub < 4, sub, sub + 8)
    outer = jnp.sum(jnp.where(lane == place + 16 * j, edge, 0.0), axis=1, keepdims=True)
    return jnp.concatenate([unpack_col(mid, j), outer], axis=0)


def ring_field(own, below, above, left, right):
    sub = iota((8, LANES), 0)
    main = jnp.concatenate([own, jnp.where(sub < 4, below, above)], axis=0)
    lane = iota((RING, LANES), 1)
    rim = jnp.zeros((RING, LANES), F32)
    for j in range(3):
        rim = jnp.where(lane == 125 + j, unpack_rim(*left, j), rim)
        rim = jnp.where(lane == j, unpack_rim(*right, j), rim)
    return jnp.concatenate([main, rim], axis=1)


def up(x):
    return pltpu.roll(x, 1, axis=0)


def down(x):
    return pltpu.roll(x, x.shape[0] - 1, axis=0)


def left_of(x):
    return pltpu.roll(x, 1, axis=1)


def right_of(x):
    return pltpu.roll(x, x.shape[1] - 1, axis=1)


def sweep(here, above, heat, is_last, is_first, inside, friction, rows, width):
    a, b = here
    has_above = 1.0 - is_last
    has_below = 1.0 - is_first
    (au, bu), (ad, bd) = above
    aN, aS, aW, aE = up(a), down(a), left_of(a), right_of(a)
    bN, bS, bW, bE = up(b), down(b), left_of(b), right_of(b)
    ux, uy = 0.5 * (aS - aN), 0.5 * (aE - aW)
    vx, vy = 0.5 * (bS - bN), 0.5 * (bE - bW)
    uz, vz = au - a, bu - b
    shear = uy + vx
    eps2 = ux * ux + vy * vy + ux * vy + 0.25 * (shear * shear) + 0.25 * (uz * uz + vz * vz)
    eta = jnp.exp(0.25 * heat - jnp.log(eps2 + 0.01) * (1.0 / 3.0)) * inside
    cut = lambda x: x[:rows, :width]
    c = cut(eta)
    diag = c * (has_above + has_below) + friction
    up_c, down_c = c * has_above, c * has_below
    sx = up_c * cut(au) + down_c * cut(ad)
    sy = up_c * cut(bu) + down_c * cut(bd)
    for e, x, y in (
        (up(eta), aN, bN),
        (down(eta), aS, bS),
        (left_of(eta), aW, bW),
        (right_of(eta), aE, bE),
    ):
        face = 0.5 * (c + cut(e))
        diag = diag + face
        sx = sx + face * cut(x)
        sy = sy + face * cut(y)
    return sx, sy, diag, c * cut(eps2)


def kernel(
    NW,
    NN,
    ice_x,
    ice_y,
    ice_t,
    oce_x,
    oce_y,
    oce_t,
    thick_in,
    ground_in,
    wet_in,
    ice_links_in,
    ocean_links_in,
    ice_out,
    ocean_out,
    thick_out,
    melt_out,
    thick_ref,
    ground_ref,
    wet_ref,
    ice_links,
    ocean_links,
    E,
    rowbuf,
    oc,
    ipack,
    irecv,
    opack,
    orecv,
    quilt,
    iquilt,
    msg,
    msg_recv,
    msg3,
    msg3_recv,
    gw_recv,
    t_recv,
    table,
    arrived,
    table2,
    arrived2,
    weights,
    SX,
    SY,
    RD,
    local_sem,
    near_send,
    near_recv,
    a2a_send,
    a2a_recv,
    a2a_send2,
    a2a_recv2,
):
    w = lax.axis_index("wide")
    n = lax.axis_index("narrow")
    wp, wm = lax.rem(w + 1, NW), lax.rem(w + NW - 1, NW)
    np_, nm = lax.rem(n + 1, NN), lax.rem(n + NN - 1, NN)
    wide_of = {-1: wm, 0: w, 1: wp}
    ices = (ice_x, ice_y, ice_t)
    oces = (oce_x, oce_y, oce_t)

    barrier = pltpu.get_barrier_semaphore()

    def greet(i, carry):
        pl.semaphore_signal(
            barrier, 1, device_id={"wide": lax.rem(w + i, NW), "narrow": n}, device_id_type=MESH
        )
        return carry

    has_n, has_s, has_w, has_e = w > 0, w < NW - 1, n > 0, n < NN - 1
    row_ok = {-1: has_n, 0: None, 1: has_s}

    def both(x, y):
        return x if y is None else x & y

    greeted = jnp.int32(NW - 1)
    for nb, ok in ((nm, has_w), (np_, has_e)):
        for dw in (0, -1, 1):
            here = both(ok, row_ok[dw])

            @pl.when(here)
            def _(dw=dw, nb=nb):
                pl.semaphore_signal(
                    barrier, 1, device_id={"wide": wide_of[dw], "narrow": nb}, device_id_type=MESH
                )

            greeted = greeted + jnp.where(here, 1, 0)
    lax.fori_loop(1, NW, greet, 0)

    loads = []
    for f in range(3):
        loads.append(pltpu.make_async_copy(oces[f], oc.at[pl.ds(f * 180 + 10, 160)], local_sem.at[f]))
    for f in range(3):
        loads.append(
            pltpu.make_async_copy(
                ices[f],
                E.at[pl.ds(f * LAYERS, LAYERS), pl.ds(0, ROWS), pl.ds(0, LANES)],
                local_sem.at[3 + f],
            )
        )
    small = []
    for i, (src, dst) in enumerate(
        (
            (thick_in, thick_ref),
            (ground_in, ground_ref),
            (wet_in, wet_ref),
            (ice_links_in, ice_links),
            (ocean_links_in, ocean_links),
        )
    ):
        small.append(pltpu.make_async_copy(src, dst, local_sem.at[6 + i]))
    for load in small + [loads[2], loads[0], loads[1]] + loads[3:]:
        load.start()

    def blank(ref, start, count):
        ref[pl.ds(start, count)] = jnp.zeros((count,) + ref.shape[1:], ref.dtype)

    for side, ok in ((0, has_w), (1, has_e)):

        @pl.when(jnp.logical_not(ok))
        def _(side=side):
            blank(msg_recv, 3 * side, 3)
            blank(msg3_recv, 3 * side, 3)
            blank(orecv, side, 1)
            blank(irecv, 3 * side, 3)

    for side, ok in ((0, has_n), (1, has_s)):

        @pl.when(jnp.logical_not(ok))
        def _(side=side):
            for f in range(3):
                blank(oc, f * 180 + 170 * side, 10)
            blank(rowbuf, 3 * side, 3)
            blank(gw_recv, side, 1)
            blank(gw_recv, 2 + side, 1)
            blank(t_recv, side, 1)
            for k in (0, 3):
                blank(msg_recv, k + 2 * side, 1)
                blank(msg3_recv, k + 2 * side, 1)
                blank(irecv, k + 2 * side, 1)

    for load in small:
        load.wait()

    grounded = ground_ref[...].astype(F32)
    wet = wet_ref[...].astype(F32)
    thick = thick_ref[...]
    draft = 0.9 * thick * (1.0 - grounded)

    def build_table(dst, at, values, links):
        dest = iota((NW, LANES), 0)
        acc = jnp.zeros((NW, LANES), F32)
        for q in range(ROWS):
            hit = dest == (links[q] >> 4)
            acc = jnp.where(hit, jnp.broadcast_to(values[q : q + 1, :], (NW, LANES)), acc)
        dst[:, :, pl.ds(at, LANES)] = acc.reshape(NW, 1, LANES)

    def gather(src, at, links):
        rows = []
        for q in range(ROWS):
            link = links[q]
            row = src[jnp.maximum(link, 0) >> 4, :, pl.ds(at, LANES)]
            rows.append(jnp.where(jnp.full((1, LANES), link, jnp.int32) >= 0, row, 0.0))
        return jnp.concatenate(rows, axis=0)

    loads[2].wait()
    t0 = jnp.concatenate([oc[360 + 10 + 10 * r, 0:1, :] for r in range(ROWS)], axis=0)
    msg[0] = pack_cols([(t0, 127), (wet, 127), (grounded, 125), (grounded, 126), (grounded, 127)])
    msg[1] = pack_cols([(t0, 0), (wet, 0), (grounded, 0), (grounded, 1), (grounded, 2)])

    lane8 = iota((8, LANES), 1)
    pl.semaphore_wait(barrier, greeted)

    near = []

    def send(src, dst, device, goes, comes):
        k = len(near)
        copy = pltpu.make_async_remote_copy(
            src_ref=src,
            dst_ref=dst,
            send_sem=near_send.at[k],
            recv_sem=near_recv.at[k],
            device_id=device,
            device_id_type=MESH,
        )
        pl.when(goes)(lambda: copy.start())
        near.append((copy, goes))
        return copy, comes

    def release(copies):
        for copy, goes in copies:
            pl.when(goes)(lambda copy=copy: copy.wait_send())

    def receive(copies):
        for copy, comes in copies:
            pl.when(comes)(lambda copy=copy: copy.wait_recv())

    def east(dw):
        device = {"wide": wide_of[dw], "narrow": np_}
        return device, both(has_e, row_ok[dw]), both(has_w, row_ok[-dw])

    def west(dw):
        device = {"wide": wide_of[dw], "narrow": nm}
        return device, both(has_w, row_ok[dw]), both(has_e, row_ok[-dw])

    south = {"wide": wp, "narrow": n}, has_s, has_n
    north = {"wide": wm, "narrow": n}, has_n, has_s

    edges = []
    for dw in (0, 1, -1):
        edges.append(send(msg.at[0], msg_recv.at[1 - dw], *east(dw)))
        edges.append(send(msg.at[1], msg_recv.at[3 + 1 - dw], *west(dw)))

    def exchange(src, dst, send_sem, recv_sem):
        def one(i, carry):
            d = lax.rem(w + i, NW)
            pltpu.make_async_remote_copy(
                src_ref=src.at[d],
                dst_ref=dst.at[w],
                send_sem=send_sem,
                recv_sem=recv_sem,
                device_id={"wide": d, "narrow": n},
                device_id_type=MESH,
            ).start()
            return carry

        lax.fori_loop(1, NW, one, 0)

    def settle(src, dst, send_sem, recv_sem, sending):
        copy = pltpu.make_async_remote_copy(
            src_ref=src.at[pl.ds(0, NW - 1)],
            dst_ref=dst.at[pl.ds(0, NW - 1)],
            send_sem=send_sem,
            recv_sem=recv_sem,
            device_id={"wide": wp, "narrow": n},
            device_id_type=MESH,
        )
        if sending:
            copy.wait_send()
        else:
            copy.wait_recv()

    ocean_rows = []
    ocean_rows.append(send(oces[2].at[pl.ds(150, 10)], oc.at[pl.ds(360, 10)], *south))
    ocean_rows.append(send(oces[2].at[pl.ds(0, 10)], oc.at[pl.ds(360 + 170, 10)], *north))
    mask_rows = []
    for j, ref in ((0, ground_ref), (1, wet_ref)):
        mask_rows.append(send(ref.at[pl.ds(8, 8)], gw_recv.at[2 * j], *south))
        mask_rows.append(send(ref.at[pl.ds(0, 8)], gw_recv.at[2 * j + 1], *north))
    ice_rows = []
    for f in range(3):
        ice_rows.append(send(ices[f].at[:, pl.ds(8, 8), :], rowbuf.at[f], *south))
        ice_rows.append(send(ices[f].at[:, pl.ds(0, 8), :], rowbuf.at[3 + f], *north))
    build_table(table, 0, draft, ice_links)
    build_table(table, LANES, wet, ocean_links)
    arrived[w] = table[w]

    exchange(table, arrived, a2a_send, a2a_recv)
    for f in range(2):
        ocean_rows.append(send(oces[f].at[pl.ds(150, 10)], oc.at[pl.ds(f * 180, 10)], *south))
        ocean_rows.append(send(oces[f].at[pl.ds(0, 10)], oc.at[pl.ds(f * 180 + 170, 10)], *north))


    for load in loads[3:]:
        load.wait()

    def pack_ice(j, accs):
        out = []
        for v in range(4):
            k = v * 16 + j
            if v == 3:
                k = jnp.minimum(k, 59)
            x = E[k // 2, pl.ds(pl.multiple_of(8 * (k % 2), 8), 8), pl.ds(0, LANES)]
            out.append(jnp.where((lane8 >> 3) == j, pltpu.roll(x, 8 * j + 4, axis=1), accs[v]))
        return tuple(out)

    inter = lax.fori_loop(0, 16, pack_ice, tuple(jnp.zeros((8, LANES), F32) for _ in range(4)))
    low = (lane8 & 7) < 4
    for v in range(2):
        p0, p1 = inter[2 * v], inter[2 * v + 1]
        ipack[0, v] = jnp.where(low, p0, pltpu.roll(p1, 4, axis=1))
        ipack[1, v] = jnp.where(low, pltpu.roll(p0, LANES - 4, axis=1), p1)

    ice_cols = []
    for dw in (0, 1, -1):
        ice_cols.append(send(ipack.at[0], irecv.at[1 - dw], *east(dw)))
        ice_cols.append(send(ipack.at[1], irecv.at[3 + 1 - dw], *west(dw)))

    for load in loads[:2]:
        load.wait()

    def pack_ocean(j, accs):
        out = []
        for v in range(8):
            k = v * 64 + j
            if v == 7:
                k = jnp.minimum(k, 479)
            x = oc[k + 20 * (k // 160) + 10]
            out.append(jnp.where((lane8 >> 1) == j, pltpu.roll(x, 2 * j + 1, axis=1), accs[v]))
        return tuple(out)

    inter = lax.fori_loop(0, 64, pack_ocean, tuple(jnp.zeros((8, LANES), F32) for _ in range(8)))
    even = (lane8 & 1) == 0
    for v in range(4):
        p0, p1 = inter[2 * v], inter[2 * v + 1]
        opack[0, v] = jnp.where(even, p0, pltpu.roll(p1, 1, axis=1))
        opack[1, v] = jnp.where(even, pltpu.roll(p0, LANES - 1, axis=1), p1)

    ocean_cols = [send(opack.at[0], orecv.at[0], *east(0)), send(opack.at[1], orecv.at[1], *west(0))]

    ring_row = iota((RING, WIDTH), 0)
    ring_col = iota((RING, WIDTH), 1)
    global_row = w * ROWS + jnp.where(ring_row < 20, ring_row, ring_row - RING)
    global_col = n * LANES + jnp.where(ring_col < 192, ring_col, ring_col - WIDTH)
    good = (global_row >= 0) & (global_row < NW * ROWS) & (global_col >= 0) & (global_col < NN * LANES)
    inside = jnp.where(good, 1.0, 0.0)

    receive(ice_rows)
    sub8 = iota((8, LANES), 0)
    edge_in = inside[16:24, 0:LANES]
    for f in range(3):
        def stitch(l, carry, f=f):
            merged = jnp.where(sub8 < 4, rowbuf[3 + f, l], rowbuf[f, l])
            E[f * LAYERS + l, pl.ds(16, 8), pl.ds(0, LANES)] = merged * edge_in
            return carry

        lax.fori_loop(0, LAYERS, stitch, 0)

    receive(mask_rows + ocean_rows[:2] + edges)
    g_below, g_above = gw_recv[1].astype(F32), gw_recv[0].astype(F32)
    w_below, w_above = gw_recv[3].astype(F32), gw_recv[2].astype(F32)
    left_msgs = (msg_recv[1], msg_recv[2], msg_recv[0])
    right_msgs = (msg_recv[4], msg_recv[5], msg_recv[3])

    row16 = iota((ROWS, LANES), 0)
    lane16 = iota((ROWS, LANES), 1)
    def four(x, first, last, west_col, east_col):
        north_x = jnp.where(row16 == 0, jnp.broadcast_to(first, (ROWS, LANES)), up(x))
        south_x = jnp.where(row16 == 15, jnp.broadcast_to(last, (ROWS, LANES)), down(x))
        west_x = jnp.where(lane16 == 0, west_col, left_of(x))
        east_x = jnp.where(lane16 == 127, east_col, right_of(x))
        return north_x, south_x, west_x, east_x

    wet_four = four(
        wet,
        w_above[7:8, :],
        w_below[0:1, :],
        unpack_col(left_msgs[0], 1),
        unpack_col(right_msgs[0], 1),
    )
    t_four = four(
        t0,
        oc[360, 0:1, :],
        oc[360 + 170, 0:1, :],
        unpack_col(left_msgs[0], 0),
        unpack_col(right_msgs[0], 0),
    )
    t_mixed = t0
    for i in range(4):
        weight = 0.2 * (wet * wet_four[i])
        weights[i] = weight
        t_mixed = t_mixed + weight * (t_four[i] - t0)

    build_table(table2, 0, t_mixed, ocean_links)
    arrived2[w] = table2[w]
    exchange(table2, arrived2, a2a_send2, a2a_recv2)

    ground24 = ring_field(
        grounded,
        g_below,
        g_above,
        *[
            tuple(pltpu.roll(m, LANES - 32, axis=1) for m in msgs)
            for msgs in (left_msgs, right_msgs)
        ],
    )
    friction = 0.1 + 9.9 * ground24

    receive(ice_cols)
    for t in range(3):
        for v in range(2):
            r, l = irecv[t, v], irecv[3 + t, v]
            iquilt[4 * t + 2 * v] = jnp.where(low, r, pltpu.roll(l, 4, axis=1))
            iquilt[4 * t + 2 * v + 1] = jnp.where(low, pltpu.roll(r, LANES - 4, axis=1), l)
    rim_in = inside[:, LANES:]

    def unpack_ice(fl, carry):
        def piece(t, g):
            k = fl * 2 + g
            return pltpu.roll(iquilt[4 * t + k // 16], LANES - 4 - 8 * (k % 16), axis=1)

        outer = jnp.where(sub8 < 4, piece(2, 0), piece(0, 1))
        for g, x in enumerate((piece(1, 0), piece(1, 1), outer)):
            E[fl, pl.ds(8 * g, 8), pl.ds(LANES, LANES)] = x * rim_in[8 * g : 8 * g + 8, :]
        return carry

    lax.fori_loop(0, 30, unpack_ice, 0)

    def first_sweep(l, carry):
        lu, ld = jnp.minimum(l + 1, LAYERS - 1), jnp.maximum(l - 1, 0)
        is_last = jnp.where(l == LAYERS - 1, 1.0, 0.0)
        is_first = jnp.where(l == 0, 1.0, 0.0)
        sx, sy, diag, _ = sweep(
            (E[l], E[LAYERS + l]),
            ((E[lu], E[LAYERS + lu]), (E[ld], E[LAYERS + ld])),
            E[2 * LAYERS + l],
            is_last,
            is_first,
            inside,
            friction,
            RING,
            WIDTH,
        )
        SX[l] = sx
        SY[l] = sy
        RD[l] = inside / diag
        return carry

    lax.fori_loop(0, LAYERS, first_sweep, 0, unroll=2)

    def linked(links):
        return jnp.concatenate(
            [jnp.where(jnp.full((1, LANES), links[q], jnp.int32) >= 0, 1.0, 0.0) for q in range(ROWS)],
            axis=0,
        )

    settle(table, arrived, a2a_send, a2a_recv, False)
    ocean_draft = gather(arrived, 0, ocean_links)
    melt_out[...] = 0.5 * (t_mixed - (0.0832 - 0.761 * ocean_draft)) * wet * linked(ocean_links)
    ice_wet = gather(arrived, LANES, ice_links) * linked(ice_links)

    settle(table2, arrived2, a2a_send2, a2a_recv2, False)
    ice_melt = 0.5 * (gather(arrived2, 0, ice_links) - (0.0832 - 0.761 * draft)) * ice_wet
    new_thick = thick - 0.05 * ice_melt * (1.0 - grounded)
    thick_out[...] = new_thick
    msg3[0] = pack_cols([(new_thick, 125), (new_thick, 126), (new_thick, 127)])
    msg3[1] = pack_cols([(new_thick, 0), (new_thick, 1), (new_thick, 2)])
    early = list(near)
    thick_edges = []
    for dw in (0, 1, -1):
        thick_edges.append(send(msg3.at[0], msg3_recv.at[1 - dw], *east(dw)))
        thick_edges.append(send(msg3.at[1], msg3_recv.at[3 + 1 - dw], *west(dw)))
    thick_edges.append(send(thick_out.at[pl.ds(8, 8)], t_recv.at[0], *south))
    thick_edges.append(send(thick_out.at[pl.ds(0, 8)], t_recv.at[1], *north))

    receive(ocean_cols + ocean_rows[2:])
    for v in range(4):
        r, l = orecv[0, v], orecv[1, v]
        quilt[2 * v] = jnp.where(even, l, pltpu.roll(r, 1, axis=1))
        quilt[2 * v + 1] = jnp.where(even, pltpu.roll(l, LANES - 1, axis=1), r)
    at_first = lane8 == 0
    at_last = lane8 == 127

    def mix_row(r, carry):
        weight = [jnp.broadcast_to(weights[i, pl.ds(r, 1), :], (8, LANES)) for i in range(4)]
        for f in range(3):
            for g in range(GROUPS):
                k = f * 160 + r * 10 + g
                at = f * 180 + 10 + r * 10 + g
                j = k % 64
                edge = pltpu.roll(quilt[k // 64], LANES - 1 - 2 * j, axis=1)
                x = oc[at]
                x_w = jnp.where(at_first, edge, pltpu.roll(x, 1, axis=1))
                x_e = jnp.where(at_last, edge, pltpu.roll(x, LANES - 1, axis=1))
                out = x + weight[0] * (oc[at - 10] - x)
                out = out + weight[1] * (oc[at + 10] - x)
                out = out + weight[2] * (x_w - x)
                out = out + weight[3] * (x_e - x)
                if f == 2 and g == 0:
                    lower = jnp.broadcast_to(melt_out[pl.ds(r, 1), :], (8, LANES))
                    out = jnp.where(sub8 == 0, out - 0.2 * lower, out)
                ocean_out[f, r * 10 + g] = out
        return carry

    lax.fori_loop(0, ROWS, mix_row, 0, unroll=2)
    release(early)
    settle(table, arrived, a2a_send, a2a_recv, True)
    settle(table2, arrived2, a2a_send2, a2a_recv2, True)

    receive(thick_edges)
    thick24 = ring_field(
        new_thick,
        t_recv[1],
        t_recv[0],
        (msg3_recv[1], msg3_recv[2], msg3_recv[0]),
        (msg3_recv[4], msg3_recv[5], msg3_recv[3]),
    )
    surface = thick24 * (0.1 + 0.9 * ground24) * inside
    stress_x = -0.05 * thick24 * (down(surface) - up(surface))
    stress_y = -0.05 * thick24 * (right_of(surface) - left_of(surface))

    def finish_first(l, carry):
        rd = RD[l]
        SX[l] = (SX[l] + stress_x) * rd
        SY[l] = (SY[l] + stress_y) * rd
        return carry

    lax.fori_loop(0, LAYERS, finish_first, 0, unroll=5)
    friction16 = friction[:ROWS, :LANES]
    stress_x16 = stress_x[:ROWS, :LANES]
    stress_y16 = stress_y[:ROWS, :LANES]

    def second_sweep(l, carry):
        lu, ld = jnp.minimum(l + 1, LAYERS - 1), jnp.maximum(l - 1, 0)
        is_last = jnp.where(l == LAYERS - 1, 1.0, 0.0)
        is_first = jnp.where(l == 0, 1.0, 0.0)
        heat = E[2 * LAYERS + l]
        sx, sy, diag, work = sweep(
            (SX[l], SY[l]),
            ((SX[lu], SY[lu]), (SX[ld], SY[ld])),
            heat,
            is_last,
            is_first,
            inside,
            friction16,
            ROWS,
            LANES,
        )
        inv = 1.0 / diag
        ice_out[0, l] = (sx + stress_x16) * inv
        ice_out[1, l] = (sy + stress_y16) * inv
        ice_out[2, l] = heat[:ROWS, :LANES] + 0.01 * work
        return carry

    lax.fori_loop(0, LAYERS, second_sweep, 0, unroll=2)

    release(near[len(early) :])


def writer(*refs):
    sources, targets, sems = refs[:4], refs[4:8], refs[8]
    copies = [pltpu.make_async_copy(sources[i], targets[i], sems.at[i]) for i in (1, 0, 2, 3)]
    for copy in copies:
        copy.start()
    for copy in copies:
        copy.wait()


def local(
    NW,
    NN,
    ice_x,
    ice_y,
    ice_temp,
    ocean_x,
    ocean_y,
    ocean_temp,
    thick,
    grounded_mask,
    wet_mask,
    ice_links,
    ocean_links,
):
    anywhere = pl.BlockSpec(memory_space=pl.ANY)
    vmem = pl.BlockSpec(memory_space=pltpu.VMEM)
    ices = [jnp.transpose(x, (1, 0, 2)) for x in (ice_x, ice_y, ice_temp)]
    oces = [x.reshape(160, 8, LANES) for x in (ocean_x, ocean_y, ocean_temp)]
    V = lambda *shape: pltpu.VMEM(shape, F32)
    D = pltpu.SemaphoreType.DMA
    shapes = ((3, LAYERS, ROWS, LANES), (3, 160, 8, LANES), (ROWS, LANES), (ROWS, LANES))
    results = pl.pallas_call(
        functools.partial(kernel, NW, NN),
        out_shape=[pltpu.VMEM(shape, F32) for shape in shapes],
        in_specs=[anywhere] * 11,
        out_specs=[vmem] * 4,
        scratch_shapes=[
            V(ROWS, LANES),
            pltpu.VMEM((ROWS, LANES), jnp.int32),
            pltpu.VMEM((ROWS, LANES), jnp.int32),
            pltpu.SMEM((ROWS,), jnp.int32),
            pltpu.SMEM((ROWS,), jnp.int32),
            V(30, RING, WIDTH),
            V(6, LAYERS, 8, LANES),
            V(540, 8, LANES),
            V(2, 2, 8, LANES),
            V(6, 2, 8, LANES),
            V(2, 4, 8, LANES),
            V(2, 4, 8, LANES),
            V(8, 8, LANES),
            V(12, 8, LANES),
            V(2, 1, LANES),
            V(6, 1, LANES),
            V(2, 1, LANES),
            V(6, 1, LANES),
            pltpu.VMEM((4, 8, LANES), jnp.int32),
            V(2, 8, LANES),
            V(NW, 1, 2 * LANES),
            V(NW, 1, 2 * LANES),
            V(NW, 1, LANES),
            V(NW, 1, LANES),
            V(4, ROWS, LANES),
            V(LAYERS, RING, WIDTH),
            V(LAYERS, RING, WIDTH),
            V(LAYERS, RING, WIDTH),
            D((11,)),
            D((40,)),
            D((40,)),
            D(()),
            D(()),
            D(()),
            D(()),
        ],
        compiler_params=pltpu.CompilerParams(collective_id=0, has_side_effects=True),
    )(
        *ices,
        *oces,
        thick,
        grounded_mask,
        wet_mask,
        ice_links.reshape(ROWS),
        ocean_links.reshape(ROWS),
    )
    ice, ocean, new_thick, melt = pl.pallas_call(
        writer,
        out_shape=[jax.ShapeDtypeStruct(shape, F32) for shape in shapes],
        in_specs=[vmem] * 4,
        out_specs=[anywhere] * 4,
        scratch_shapes=[D((4,))],
    )(*[pltpu.with_memory_space_constraint(x, pltpu.VMEM) for x in results])
    return (
        jnp.transpose(ice, (0, 2, 1, 3)),
        ocean.reshape(3, ROWS, 80, LANES),
        new_thick,
        melt,
    )


def solution(mesh):
    deep = P("wide", None, "narrow")
    flat = P("wide", "narrow")
    return jax.shard_map(
        functools.partial(local, mesh.shape["wide"], mesh.shape["narrow"]),
        mesh=mesh,
        in_specs=(deep,) * 6 + (flat,) * 5,
        out_specs=(P(None, "wide", None, "narrow"), P(None, "wide", None, "narrow"), flat, flat),
        check_vma=False,
    )
```

```python
import functools

import jax
import jax.numpy as jnp
from jax import lax
from jax.experimental import pallas as pl
from jax.experimental.pallas import tpu as pltpu
from jax.sharding import PartitionSpec as P

MESH = pl.DeviceIdType.MESH
F32 = jnp.float32

ROWS = 16
LANES = 128
LAYERS = 10
GROUPS = 10
RING = 24
WIDTH = 256


def iota(shape, dim):
    return lax.broadcasted_iota(jnp.int32, shape, dim)


def pack_cols(pieces):
    lane = iota((ROWS, LANES), 1)
    row = iota((ROWS, LANES), 0)
    acc = jnp.zeros((ROWS, LANES), F32)
    for j, (value, col) in enumerate(pieces):
        wide = jnp.broadcast_to(value[:, col : col + 1], (ROWS, LANES))
        acc = jnp.where(lane == row + 16 * j, wide, acc)
    return jnp.sum(acc, axis=0, keepdims=True)


def unpack_col(mid, j):
    lane = iota((ROWS, LANES), 1)
    row = iota((ROWS, LANES), 0)
    wide = jnp.broadcast_to(mid, (ROWS, LANES))
    return jnp.sum(jnp.where(lane == row + 16 * j, wide, 0.0), axis=1, keepdims=True)


def unpack_rim(mid, below, above, j):
    lane = iota((8, LANES), 1)
    sub = iota((8, LANES), 0)
    edge = jnp.where(sub < 4, jnp.broadcast_to(below, (8, LANES)), jnp.broadcast_to(above, (8, LANES)))
    place = jnp.where(sub < 4, sub, sub + 8)
    outer = jnp.sum(jnp.where(lane == place + 16 * j, edge, 0.0), axis=1, keepdims=True)
    return jnp.concatenate([unpack_col(mid, j), outer], axis=0)


def ring_field(own, below, above, left, right):
    sub = iota((8, LANES), 0)
    main = jnp.concatenate([own, jnp.where(sub < 4, below, above)], axis=0)
    lane = iota((RING, LANES), 1)
    rim = jnp.zeros((RING, LANES), F32)
    for j in range(3):
        rim = jnp.where(lane == 125 + j, unpack_rim(*left, j), rim)
        rim = jnp.where(lane == j, unpack_rim(*right, j), rim)
    return jnp.concatenate([main, rim], axis=1)


def up(x):
    return pltpu.roll(x, 1, axis=0)


def down(x):
    return pltpu.roll(x, x.shape[0] - 1, axis=0)


def left_of(x):
    return pltpu.roll(x, 1, axis=1)


def right_of(x):
    return pltpu.roll(x, x.shape[1] - 1, axis=1)


def sweep(here, above, heat, is_last, is_first, inside, friction, rows, width):
    a, b = here
    has_above = 1.0 - is_last
    has_below = 1.0 - is_first
    (au, bu), (ad, bd) = above
    aN, aS, aW, aE = up(a), down(a), left_of(a), right_of(a)
    bN, bS, bW, bE = up(b), down(b), left_of(b), right_of(b)
    ux, uy = 0.5 * (aS - aN), 0.5 * (aE - aW)
    vx, vy = 0.5 * (bS - bN), 0.5 * (bE - bW)
    uz, vz = au - a, bu - b
    shear = uy + vx
    eps2 = ux * ux + vy * vy + ux * vy + 0.25 * (shear * shear) + 0.25 * (uz * uz + vz * vz)
    eta = jnp.exp(0.25 * heat - jnp.log(eps2 + 0.01) * (1.0 / 3.0)) * inside
    cut = lambda x: x[:rows, :width]
    c = cut(eta)
    diag = c * (has_above + has_below) + friction
    up_c, down_c = c * has_above, c * has_below
    sx = up_c * cut(au) + down_c * cut(ad)
    sy = up_c * cut(bu) + down_c * cut(bd)
    for e, x, y in (
        (up(eta), aN, bN),
        (down(eta), aS, bS),
        (left_of(eta), aW, bW),
        (right_of(eta), aE, bE),
    ):
        face = 0.5 * (c + cut(e))
        diag = diag + face
        sx = sx + face * cut(x)
        sy = sy + face * cut(y)
    return sx, sy, diag, c * cut(eps2)


def kernel(
    NW,
    NN,
    ice_x,
    ice_y,
    ice_t,
    oce_x,
    oce_y,
    oce_t,
    thick_in,
    ground_in,
    wet_in,
    ice_links_in,
    ocean_links_in,
    ice_out,
    ocean_out,
    thick_out,
    melt_out,
    thick_ref,
    ground_ref,
    wet_ref,
    ice_links,
    ocean_links,
    E,
    rowbuf,
    oc,
    ipack,
    irecv,
    opack,
    orecv,
    quilt,
    iquilt,
    msg,
    msg_recv,
    msg3,
    msg3_recv,
    gw_recv,
    t_recv,
    table,
    arrived,
    table2,
    arrived2,
    table3,
    arrived3,
    weights,
    SX,
    SY,
    RD,
    local_sem,
    near_send,
    near_recv,
    a2a_send,
    a2a_recv,
    a2a_send2,
    a2a_recv2,
    a2a_send3,
    a2a_recv3,
):
    w = lax.axis_index("wide")
    n = lax.axis_index("narrow")
    wp, wm = lax.rem(w + 1, NW), lax.rem(w + NW - 1, NW)
    np_, nm = lax.rem(n + 1, NN), lax.rem(n + NN - 1, NN)
    wide_of = {-1: wm, 0: w, 1: wp}
    ices = (ice_x, ice_y, ice_t)
    oces = (oce_x, oce_y, oce_t)

    barrier = pltpu.get_barrier_semaphore()

    def greet(i, carry):
        pl.semaphore_signal(
            barrier, 1, device_id={"wide": lax.rem(w + i, NW), "narrow": n}, device_id_type=MESH
        )
        return carry

    has_n, has_s, has_w, has_e = w > 0, w < NW - 1, n > 0, n < NN - 1
    row_ok = {-1: has_n, 0: None, 1: has_s}

    def both(x, y):
        return x if y is None else x & y

    greeted = jnp.int32(NW - 1)
    for nb, ok in ((nm, has_w), (np_, has_e)):
        for dw in (0, -1, 1):
            here = both(ok, row_ok[dw])

            @pl.when(here)
            def _(dw=dw, nb=nb):
                pl.semaphore_signal(
                    barrier, 1, device_id={"wide": wide_of[dw], "narrow": nb}, device_id_type=MESH
                )

            greeted = greeted + jnp.where(here, 1, 0)
    lax.fori_loop(1, NW, greet, 0)

    loads = []
    for f in range(3):
        loads.append(pltpu.make_async_copy(oces[f], oc.at[pl.ds(f * 180 + 10, 160)], local_sem.at[f]))
    for f in range(3):
        loads.append(
            pltpu.make_async_copy(
                ices[f],
                E.at[pl.ds(f * LAYERS, LAYERS), pl.ds(0, ROWS), pl.ds(0, LANES)],
                local_sem.at[3 + f],
            )
        )
    small = []
    for i, (src, dst) in enumerate(
        (
            (thick_in, thick_ref),
            (ground_in, ground_ref),
            (wet_in, wet_ref),
            (ice_links_in, ice_links),
            (ocean_links_in, ocean_links),
        )
    ):
        small.append(pltpu.make_async_copy(src, dst, local_sem.at[6 + i]))
    for load in small + [loads[2], loads[0], loads[1]] + loads[3:]:
        load.start()

    def blank(ref, start, count):
        ref[pl.ds(start, count)] = jnp.zeros((count,) + ref.shape[1:], ref.dtype)

    for side, ok in ((0, has_w), (1, has_e)):

        @pl.when(jnp.logical_not(ok))
        def _(side=side):
            blank(msg_recv, 3 * side, 3)
            blank(msg3_recv, 3 * side, 3)
            blank(orecv, side, 1)
            blank(irecv, 3 * side, 3)

    for side, ok in ((0, has_n), (1, has_s)):

        @pl.when(jnp.logical_not(ok))
        def _(side=side):
            for f in range(3):
                blank(oc, f * 180 + 170 * side, 10)
            blank(rowbuf, 3 * side, 3)
            blank(gw_recv, side, 1)
            blank(gw_recv, 2 + side, 1)
            blank(t_recv, side, 1)
            for k in (0, 3):
                blank(msg_recv, k + 2 * side, 1)
                blank(msg3_recv, k + 2 * side, 1)
                blank(irecv, k + 2 * side, 1)

    for load in small:
        load.wait()

    grounded = ground_ref[...].astype(F32)
    wet = wet_ref[...].astype(F32)
    thick = thick_ref[...]
    draft = 0.9 * thick * (1.0 - grounded)

    def build_table(dst, at, values, links):
        dest = iota((NW, LANES), 0)
        acc = jnp.zeros((NW, LANES), F32)
        for q in range(ROWS):
            hit = dest == (links[q] >> 4)
            acc = jnp.where(hit, jnp.broadcast_to(values[q : q + 1, :], (NW, LANES)), acc)
        dst[:, :, pl.ds(at, LANES)] = acc.reshape(NW, 1, LANES)

    def gather(src, at, links):
        rows = []
        for q in range(ROWS):
            link = links[q]
            row = src[jnp.maximum(link, 0) >> 4, :, pl.ds(at, LANES)]
            rows.append(jnp.where(jnp.full((1, LANES), link, jnp.int32) >= 0, row, 0.0))
        return jnp.concatenate(rows, axis=0)

    loads[2].wait()
    t0 = jnp.concatenate([oc[360 + 10 + 10 * r, 0:1, :] for r in range(ROWS)], axis=0)
    msg[0] = pack_cols([(t0, 127), (wet, 127), (grounded, 125), (grounded, 126), (grounded, 127)])
    msg[1] = pack_cols([(t0, 0), (wet, 0), (grounded, 0), (grounded, 1), (grounded, 2)])

    lane8 = iota((8, LANES), 1)
    pl.semaphore_wait(barrier, greeted)

    near = []

    def send(src, dst, device, goes, comes):
        k = len(near)
        copy = pltpu.make_async_remote_copy(
            src_ref=src,
            dst_ref=dst,
            send_sem=near_send.at[k],
            recv_sem=near_recv.at[k],
            device_id=device,
            device_id_type=MESH,
        )
        pl.when(goes)(lambda: copy.start())
        near.append((copy, goes))
        return copy, comes

    def release(copies):
        for copy, goes in copies:
            pl.when(goes)(lambda copy=copy: copy.wait_send())

    def receive(copies):
        for copy, comes in copies:
            pl.when(comes)(lambda copy=copy: copy.wait_recv())

    def east(dw):
        device = {"wide": wide_of[dw], "narrow": np_}
        return device, both(has_e, row_ok[dw]), both(has_w, row_ok[-dw])

    def west(dw):
        device = {"wide": wide_of[dw], "narrow": nm}
        return device, both(has_w, row_ok[dw]), both(has_e, row_ok[-dw])

    south = {"wide": wp, "narrow": n}, has_s, has_n
    north = {"wide": wm, "narrow": n}, has_n, has_s

    edges = []
    for dw in (0, 1, -1):
        edges.append(send(msg.at[0], msg_recv.at[1 - dw], *east(dw)))
        edges.append(send(msg.at[1], msg_recv.at[3 + 1 - dw], *west(dw)))

    def exchange(src, dst, send_sem, recv_sem):
        def one(i, carry):
            d = lax.rem(w + i, NW)
            pltpu.make_async_remote_copy(
                src_ref=src.at[d],
                dst_ref=dst.at[w],
                send_sem=send_sem,
                recv_sem=recv_sem,
                device_id={"wide": d, "narrow": n},
                device_id_type=MESH,
            ).start()
            return carry

        lax.fori_loop(1, NW, one, 0)

    def settle(src, dst, send_sem, recv_sem, sending):
        copy = pltpu.make_async_remote_copy(
            src_ref=src.at[pl.ds(0, NW - 1)],
            dst_ref=dst.at[pl.ds(0, NW - 1)],
            send_sem=send_sem,
            recv_sem=recv_sem,
            device_id={"wide": wp, "narrow": n},
            device_id_type=MESH,
        )
        if sending:
            copy.wait_send()
        else:
            copy.wait_recv()

    ocean_rows = []
    ocean_rows.append(send(oces[2].at[pl.ds(150, 10)], oc.at[pl.ds(360, 10)], *south))
    ocean_rows.append(send(oces[2].at[pl.ds(0, 10)], oc.at[pl.ds(360 + 170, 10)], *north))
    mask_rows = []
    for j, ref in ((0, ground_ref), (1, wet_ref)):
        mask_rows.append(send(ref.at[pl.ds(8, 8)], gw_recv.at[2 * j], *south))
        mask_rows.append(send(ref.at[pl.ds(0, 8)], gw_recv.at[2 * j + 1], *north))
    ice_rows = []
    for f in range(3):
        ice_rows.append(send(ices[f].at[:, pl.ds(8, 8), :], rowbuf.at[f], *south))
        ice_rows.append(send(ices[f].at[:, pl.ds(0, 8), :], rowbuf.at[3 + f], *north))
    build_table(table, 0, wet, ocean_links)
    arrived[w] = table[w]

    exchange(table, arrived, a2a_send, a2a_recv)
    for f in range(2):
        ocean_rows.append(send(oces[f].at[pl.ds(150, 10)], oc.at[pl.ds(f * 180, 10)], *south))
        ocean_rows.append(send(oces[f].at[pl.ds(0, 10)], oc.at[pl.ds(f * 180 + 170, 10)], *north))


    for load in loads[3:]:
        load.wait()

    def pack_ice(j, accs):
        out = []
        for v in range(4):
            k = v * 16 + j
            if v == 3:
                k = jnp.minimum(k, 59)
            x = E[k // 2, pl.ds(pl.multiple_of(8 * (k % 2), 8), 8), pl.ds(0, LANES)]
            out.append(jnp.where((lane8 >> 3) == j, pltpu.roll(x, 8 * j + 4, axis=1), accs[v]))
        return tuple(out)

    inter = lax.fori_loop(0, 16, pack_ice, tuple(jnp.zeros((8, LANES), F32) for _ in range(4)))
    low = (lane8 & 7) < 4
    for v in range(2):
        p0, p1 = inter[2 * v], inter[2 * v + 1]
        ipack[0, v] = jnp.where(low, p0, pltpu.roll(p1, 4, axis=1))
        ipack[1, v] = jnp.where(low, pltpu.roll(p0, LANES - 4, axis=1), p1)

    ice_cols = []
    for dw in (0, 1, -1):
        ice_cols.append(send(ipack.at[0], irecv.at[1 - dw], *east(dw)))
        ice_cols.append(send(ipack.at[1], irecv.at[3 + 1 - dw], *west(dw)))

    for load in loads[:2]:
        load.wait()

    def pack_ocean(j, accs):
        out = []
        for v in range(8):
            k = v * 64 + j
            if v == 7:
                k = jnp.minimum(k, 479)
            x = oc[k + 20 * (k // 160) + 10]
            out.append(jnp.where((lane8 >> 1) == j, pltpu.roll(x, 2 * j + 1, axis=1), accs[v]))
        return tuple(out)

    inter = lax.fori_loop(0, 64, pack_ocean, tuple(jnp.zeros((8, LANES), F32) for _ in range(8)))
    even = (lane8 & 1) == 0
    for v in range(4):
        p0, p1 = inter[2 * v], inter[2 * v + 1]
        opack[0, v] = jnp.where(even, p0, pltpu.roll(p1, 1, axis=1))
        opack[1, v] = jnp.where(even, pltpu.roll(p0, LANES - 1, axis=1), p1)

    ocean_cols = [send(opack.at[0], orecv.at[0], *east(0)), send(opack.at[1], orecv.at[1], *west(0))]

    ring_row = iota((RING, WIDTH), 0)
    ring_col = iota((RING, WIDTH), 1)
    global_row = w * ROWS + jnp.where(ring_row < 20, ring_row, ring_row - RING)
    global_col = n * LANES + jnp.where(ring_col < 192, ring_col, ring_col - WIDTH)
    good = (global_row >= 0) & (global_row < NW * ROWS) & (global_col >= 0) & (global_col < NN * LANES)
    inside = jnp.where(good, 1.0, 0.0)

    receive(mask_rows + ocean_rows[:2] + edges)
    g_below, g_above = gw_recv[1].astype(F32), gw_recv[0].astype(F32)
    w_below, w_above = gw_recv[3].astype(F32), gw_recv[2].astype(F32)
    left_msgs = (msg_recv[1], msg_recv[2], msg_recv[0])
    right_msgs = (msg_recv[4], msg_recv[5], msg_recv[3])

    row16 = iota((ROWS, LANES), 0)
    lane16 = iota((ROWS, LANES), 1)
    def four(x, first, last, west_col, east_col):
        north_x = jnp.where(row16 == 0, jnp.broadcast_to(first, (ROWS, LANES)), up(x))
        south_x = jnp.where(row16 == 15, jnp.broadcast_to(last, (ROWS, LANES)), down(x))
        west_x = jnp.where(lane16 == 0, west_col, left_of(x))
        east_x = jnp.where(lane16 == 127, east_col, right_of(x))
        return north_x, south_x, west_x, east_x

    wet_four = four(
        wet,
        w_above[7:8, :],
        w_below[0:1, :],
        unpack_col(left_msgs[0], 1),
        unpack_col(right_msgs[0], 1),
    )
    t_four = four(
        t0,
        oc[360, 0:1, :],
        oc[360 + 170, 0:1, :],
        unpack_col(left_msgs[0], 0),
        unpack_col(right_msgs[0], 0),
    )
    t_mixed = t0
    for i in range(4):
        weight = 0.2 * (wet * wet_four[i])
        weights[i] = weight
        t_mixed = t_mixed + weight * (t_four[i] - t0)

    build_table(table2, 0, t_mixed, ocean_links)
    arrived2[w] = table2[w]
    exchange(table2, arrived2, a2a_send2, a2a_recv2)
    build_table(table3, 0, draft, ice_links)
    arrived3[w] = table3[w]
    exchange(table3, arrived3, a2a_send3, a2a_recv3)

    receive(ice_rows)
    sub8 = iota((8, LANES), 0)
    edge_in = inside[16:24, 0:LANES]
    for f in range(3):
        def stitch(l, carry, f=f):
            merged = jnp.where(sub8 < 4, rowbuf[3 + f, l], rowbuf[f, l])
            E[f * LAYERS + l, pl.ds(16, 8), pl.ds(0, LANES)] = merged * edge_in
            return carry

        lax.fori_loop(0, LAYERS, stitch, 0)


    ground24 = ring_field(
        grounded,
        g_below,
        g_above,
        *[
            tuple(pltpu.roll(m, LANES - 32, axis=1) for m in msgs)
            for msgs in (left_msgs, right_msgs)
        ],
    )
    friction = 0.1 + 9.9 * ground24

    receive(ice_cols)
    for t in range(3):
        for v in range(2):
            r, l = irecv[t, v], irecv[3 + t, v]
            iquilt[4 * t + 2 * v] = jnp.where(low, r, pltpu.roll(l, 4, axis=1))
            iquilt[4 * t + 2 * v + 1] = jnp.where(low, pltpu.roll(r, LANES - 4, axis=1), l)
    rim_in = inside[:, LANES:]

    def unpack_ice(fl, carry):
        def piece(t, g):
            k = fl * 2 + g
            return pltpu.roll(iquilt[4 * t + k // 16], LANES - 4 - 8 * (k % 16), axis=1)

        outer = jnp.where(sub8 < 4, piece(2, 0), piece(0, 1))
        for g, x in enumerate((piece(1, 0), piece(1, 1), outer)):
            E[fl, pl.ds(8 * g, 8), pl.ds(LANES, LANES)] = x * rim_in[8 * g : 8 * g + 8, :]
        return carry

    lax.fori_loop(0, 30, unpack_ice, 0)

    def first_sweep(l, carry):
        lu, ld = jnp.minimum(l + 1, LAYERS - 1), jnp.maximum(l - 1, 0)
        is_last = jnp.where(l == LAYERS - 1, 1.0, 0.0)
        is_first = jnp.where(l == 0, 1.0, 0.0)
        sx, sy, diag, _ = sweep(
            (E[l], E[LAYERS + l]),
            ((E[lu], E[LAYERS + lu]), (E[ld], E[LAYERS + ld])),
            E[2 * LAYERS + l],
            is_last,
            is_first,
            inside,
            friction,
            RING,
            WIDTH,
        )
        SX[l] = sx
        SY[l] = sy
        RD[l] = inside / diag
        return carry

    lax.fori_loop(0, LAYERS, first_sweep, 0, unroll=2)

    def linked(links):
        return jnp.concatenate(
            [jnp.where(jnp.full((1, LANES), links[q], jnp.int32) >= 0, 1.0, 0.0) for q in range(ROWS)],
            axis=0,
        )

    settle(table, arrived, a2a_send, a2a_recv, False)
    ice_wet = gather(arrived, 0, ice_links) * linked(ice_links)

    settle(table2, arrived2, a2a_send2, a2a_recv2, False)
    ice_melt = 0.5 * (gather(arrived2, 0, ice_links) - (0.0832 - 0.761 * draft)) * ice_wet
    new_thick = thick - 0.05 * ice_melt * (1.0 - grounded)
    thick_out[...] = new_thick
    msg3[0] = pack_cols([(new_thick, 125), (new_thick, 126), (new_thick, 127)])
    msg3[1] = pack_cols([(new_thick, 0), (new_thick, 1), (new_thick, 2)])
    early = list(near)
    thick_edges = []
    for dw in (0, 1, -1):
        thick_edges.append(send(msg3.at[0], msg3_recv.at[1 - dw], *east(dw)))
        thick_edges.append(send(msg3.at[1], msg3_recv.at[3 + 1 - dw], *west(dw)))
    thick_edges.append(send(thick_out.at[pl.ds(8, 8)], t_recv.at[0], *south))
    thick_edges.append(send(thick_out.at[pl.ds(0, 8)], t_recv.at[1], *north))

    settle(table3, arrived3, a2a_send3, a2a_recv3, False)
    ocean_draft = gather(arrived3, 0, ocean_links)
    melt_out[...] = 0.5 * (t_mixed - (0.0832 - 0.761 * ocean_draft)) * wet * linked(ocean_links)
    receive(ocean_cols + ocean_rows[2:])
    for v in range(4):
        r, l = orecv[0, v], orecv[1, v]
        quilt[2 * v] = jnp.where(even, l, pltpu.roll(r, 1, axis=1))
        quilt[2 * v + 1] = jnp.where(even, pltpu.roll(l, LANES - 1, axis=1), r)
    at_first = lane8 == 0
    at_last = lane8 == 127

    def mix_row(r, carry):
        weight = [jnp.broadcast_to(weights[i, pl.ds(r, 1), :], (8, LANES)) for i in range(4)]
        for f in range(3):
            for g in range(GROUPS):
                k = f * 160 + r * 10 + g
                at = f * 180 + 10 + r * 10 + g
                j = k % 64
                edge = pltpu.roll(quilt[k // 64], LANES - 1 - 2 * j, axis=1)
                x = oc[at]
                x_w = jnp.where(at_first, edge, pltpu.roll(x, 1, axis=1))
                x_e = jnp.where(at_last, edge, pltpu.roll(x, LANES - 1, axis=1))
                out = x + weight[0] * (oc[at - 10] - x)
                out = out + weight[1] * (oc[at + 10] - x)
                out = out + weight[2] * (x_w - x)
                out = out + weight[3] * (x_e - x)
                if f == 2 and g == 0:
                    lower = jnp.broadcast_to(melt_out[pl.ds(r, 1), :], (8, LANES))
                    out = jnp.where(sub8 == 0, out - 0.2 * lower, out)
                ocean_out[f, r * 10 + g] = out
        return carry

    lax.fori_loop(0, ROWS, mix_row, 0, unroll=2)
    release(early)
    settle(table, arrived, a2a_send, a2a_recv, True)
    settle(table2, arrived2, a2a_send2, a2a_recv2, True)
    settle(table3, arrived3, a2a_send3, a2a_recv3, True)

    receive(thick_edges)
    thick24 = ring_field(
        new_thick,
        t_recv[1],
        t_recv[0],
        (msg3_recv[1], msg3_recv[2], msg3_recv[0]),
        (msg3_recv[4], msg3_recv[5], msg3_recv[3]),
    )
    surface = thick24 * (0.1 + 0.9 * ground24) * inside
    stress_x = -0.05 * thick24 * (down(surface) - up(surface))
    stress_y = -0.05 * thick24 * (right_of(surface) - left_of(surface))

    def finish_first(l, carry):
        rd = RD[l]
        SX[l] = (SX[l] + stress_x) * rd
        SY[l] = (SY[l] + stress_y) * rd
        return carry

    lax.fori_loop(0, LAYERS, finish_first, 0, unroll=5)
    friction16 = friction[:ROWS, :LANES]
    stress_x16 = stress_x[:ROWS, :LANES]
    stress_y16 = stress_y[:ROWS, :LANES]

    def second_sweep(l, carry):
        lu, ld = jnp.minimum(l + 1, LAYERS - 1), jnp.maximum(l - 1, 0)
        is_last = jnp.where(l == LAYERS - 1, 1.0, 0.0)
        is_first = jnp.where(l == 0, 1.0, 0.0)
        heat = E[2 * LAYERS + l]
        sx, sy, diag, work = sweep(
            (SX[l], SY[l]),
            ((SX[lu], SY[lu]), (SX[ld], SY[ld])),
            heat,
            is_last,
            is_first,
            inside,
            friction16,
            ROWS,
            LANES,
        )
        inv = 1.0 / diag
        ice_out[0, l] = (sx + stress_x16) * inv
        ice_out[1, l] = (sy + stress_y16) * inv
        ice_out[2, l] = heat[:ROWS, :LANES] + 0.01 * work
        return carry

    lax.fori_loop(0, LAYERS, second_sweep, 0, unroll=2)

    release(near[len(early) :])


def writer(*refs):
    sources, targets, sems = refs[:4], refs[4:8], refs[8]
    copies = [pltpu.make_async_copy(sources[i], targets[i], sems.at[i]) for i in (1, 0, 2, 3)]
    for copy in copies:
        copy.start()
    for copy in copies:
        copy.wait()


def local(
    NW,
    NN,
    ice_x,
    ice_y,
    ice_temp,
    ocean_x,
    ocean_y,
    ocean_temp,
    thick,
    grounded_mask,
    wet_mask,
    ice_links,
    ocean_links,
):
    anywhere = pl.BlockSpec(memory_space=pl.ANY)
    vmem = pl.BlockSpec(memory_space=pltpu.VMEM)
    ices = [jnp.transpose(x, (1, 0, 2)) for x in (ice_x, ice_y, ice_temp)]
    oces = [x.reshape(160, 8, LANES) for x in (ocean_x, ocean_y, ocean_temp)]
    V = lambda *shape: pltpu.VMEM(shape, F32)
    D = pltpu.SemaphoreType.DMA
    shapes = ((3, LAYERS, ROWS, LANES), (3, 160, 8, LANES), (ROWS, LANES), (ROWS, LANES))
    results = pl.pallas_call(
        functools.partial(kernel, NW, NN),
        out_shape=[pltpu.VMEM(shape, F32) for shape in shapes],
        in_specs=[anywhere] * 11,
        out_specs=[vmem] * 4,
        scratch_shapes=[
            V(ROWS, LANES),
            pltpu.VMEM((ROWS, LANES), jnp.int32),
            pltpu.VMEM((ROWS, LANES), jnp.int32),
            pltpu.SMEM((ROWS,), jnp.int32),
            pltpu.SMEM((ROWS,), jnp.int32),
            V(30, RING, WIDTH),
            V(6, LAYERS, 8, LANES),
            V(540, 8, LANES),
            V(2, 2, 8, LANES),
            V(6, 2, 8, LANES),
            V(2, 4, 8, LANES),
            V(2, 4, 8, LANES),
            V(8, 8, LANES),
            V(12, 8, LANES),
            V(2, 1, LANES),
            V(6, 1, LANES),
            V(2, 1, LANES),
            V(6, 1, LANES),
            pltpu.VMEM((4, 8, LANES), jnp.int32),
            V(2, 8, LANES),
            V(NW, 1, LANES),
            V(NW, 1, LANES),
            V(NW, 1, LANES),
            V(NW, 1, LANES),
            V(NW, 1, LANES),
            V(NW, 1, LANES),
            V(4, ROWS, LANES),
            V(LAYERS, RING, WIDTH),
            V(LAYERS, RING, WIDTH),
            V(LAYERS, RING, WIDTH),
            D((11,)),
            D((40,)),
            D((40,)),
            D(()),
            D(()),
            D(()),
            D(()),
            D(()),
            D(()),
        ],
        compiler_params=pltpu.CompilerParams(collective_id=0, has_side_effects=True),
    )(
        *ices,
        *oces,
        thick,
        grounded_mask,
        wet_mask,
        ice_links.reshape(ROWS),
        ocean_links.reshape(ROWS),
    )
    ice, ocean, new_thick, melt = pl.pallas_call(
        writer,
        out_shape=[jax.ShapeDtypeStruct(shape, F32) for shape in shapes],
        in_specs=[vmem] * 4,
        out_specs=[anywhere] * 4,
        scratch_shapes=[D((4,))],
    )(*[pltpu.with_memory_space_constraint(x, pltpu.VMEM) for x in results])
    return (
        jnp.transpose(ice, (0, 2, 1, 3)),
        ocean.reshape(3, ROWS, 80, LANES),
        new_thick,
        melt,
    )


def solution(mesh):
    deep = P("wide", None, "narrow")
    flat = P("wide", "narrow")
    return jax.shard_map(
        functools.partial(local, mesh.shape["wide"], mesh.shape["narrow"]),
        mesh=mesh,
        in_specs=(deep,) * 6 + (flat,) * 5,
        out_specs=(P(None, "wide", None, "narrow"), P(None, "wide", None, "narrow"), flat, flat),
        check_vma=False,
    )
```
